256 devices in a mesh: ctx: 64 (over z, x, y_lo), dp: 4 (over y_hi, core).
Axes of the slice: x: 4, y: 4 (y_hi: 2, y_lo: 2; y = y_hi * 2 + y_lo), z: 8, core: 2. Of those that a mesh axis runs over, the one named last changes fastest.
Arguments:
- queries: bfloat16 [8192, 4096], P('ctx', 'dp'), may hold values from -100 to 100
- keys: bfloat16 [8192, 512], P('ctx', 'dp'), may hold values from -15 to 15
- values: bfloat16 [8192, 512], P('ctx', 'dp'), may hold values from -6 to 6
- segment_ids: int32 [8192], P('ctx'), may hold values from 0 to 3, never falling along the last dimension, each value on 1 to 4096 neighbouring positions
- cart_keys: bfloat16 [1024, 512], P('ctx', 'dp'), may hold values from -12 to 12
- cart_values: bfloat16 [1024, 512], P('ctx', 'dp'), may hold values from -6 to 6
Outputs:
- teacher_out: bfloat16 [8192, 4096], P('ctx', 'dp')
- student_out: bfloat16 [8192, 4096], P('ctx', 'dp')
- grad_keys: float32 [1024, 512], P('ctx')
- grad_values: float32 [1024, 512], P('ctx')
The draws below stay inside these ranges and needn't reach their ends.
Inputs may be any that keep to these rules, and one draw needn't show every extreme that they name: `segment_ids`: document numbers never fall along the context; each document spans 1 to 4096 positions, one exactly that many.
All inputs are finite; a program needn't handle non-finite values.
Results may differ from the reference program's by a relative error of at most 0.0085.
The reference program's roundings to bfloat16 on the way count: a program that leaves them out, or rounds other values in their place, can miss the bound.
Values may be sent and summed in bfloat16 or wider, within the bound.
A program may use at most 64 MiB of HBM per device.

```python
import math
import jax
import jax.numpy as jnp
import numpy as np
from jax import lax

HQ = 32
KVH = 4
HD = 128
SLOTS = 1024
DOCS = 4
TOK_DEV = 128
LENGTH = 8192
N_CTX = 64


def sample_all(key):
    base_keys = jnp.clip(jax.random.normal(jax.random.fold_in(key, 101), (LENGTH, KVH * HD), jnp.float32), -4.5, 4.5)
    slot_keys = jnp.clip(jax.random.normal(jax.random.fold_in(key, 102), (SLOTS, KVH * HD), jnp.float32), -4.5, 4.5)
    query_rows = jnp.clip(jax.random.normal(jax.random.fold_in(key, 103), (LENGTH, HQ * HD), jnp.float32), -4.5, 4.5)
    return (3.0 * base_keys, 2.5 * slot_keys, query_rows)


def draw_queries(key, part):
    return sample_all(key)[2].astype(jnp.bfloat16)


def draw_keys(key, part):
    return sample_all(key)[0].astype(jnp.bfloat16)


def draw_cart_keys(key, part):
    return sample_all(key)[1].astype(jnp.bfloat16)


def steps_of(stream_key, dims, split, smallest, largest):
    def one(axis_at, blocks):
        heights = jax.random.uniform(jax.random.fold_in(jax.random.fold_in(stream_key, 6), axis_at), (blocks,), jnp.float32, smallest / len(split), largest / len(split))
        return jnp.repeat(jnp.exp(heights), dims[axis_at] // blocks).reshape((-1,) + (1,) * (len(dims) - axis_at - 1))

    loudness = one(*split[0])
    for cut in split[1:]:
        loudness = loudness * one(*cut)
    return loudness


def length_profile(count, total, bound, lean):
    weights = [(1 << 20) // math.isqrt(standing ** lean) + 1 for standing in range(2, count + 1)]
    spare, counts = total - bound - (count - 1), [1] * (count - 1)
    while spare > 0:
        free = [i for i in range(count - 1) if counts[i] < bound]
        whole, budget = sum([weights[i] for i in free]), spare
        for i in free:
            extra = min(bound - counts[i], max(1, budget * weights[i] // whole), spare)
            counts[i] = counts[i] + extra
            spare = spare - extra
    return np.array([bound] + counts)


def ragged(rng, amount, total, reach, slope):
    if amount == 2:
        one = jax.random.randint(rng, (), max(1, total - reach), min(reach, total - 1) + 1)
        return jnp.stack([one, total - one])
    lengths = jnp.asarray(length_profile(amount, total, reach, slope), jnp.int32)
    couples = (amount - 1) // 2
    source_of, receiver = lengths[1:1 + 2 * couples:2], lengths[2:2 + 2 * couples:2]
    slack = jnp.minimum(source_of - 1, reach - receiver)
    moved = jax.random.randint(jax.random.fold_in(rng, 1), (couples,), 0, 1 << 20) % (slack + 1)
    lengths = lengths.at[1:1 + 2 * couples:2].set(source_of - moved).at[2:2 + 2 * couples:2].set(receiver + moved)
    return lengths[jax.random.permutation(jax.random.fold_in(rng, 2), amount)]


def noise(stream_key, dims, width, bound, pieces=(), held_as=jnp.bfloat16):
    loudness = steps_of(stream_key, dims, pieces, -0.22, 0.18) if pieces else 1.0
    result = jax.random.normal(stream_key, dims, jnp.float32) * width * loudness
    return jnp.minimum(jnp.maximum(result, -bound), bound).astype(held_as)


def setup_inputs(seed: int = 0) -> dict:
    splits = jax.random.split(jax.random.key(seed), 7)
    return {
        "queries": draw_queries(jax.random.fold_in(splits[6], 71), 0),
        "keys": draw_keys(jax.random.fold_in(splits[6], 71), 0),
        "values": noise(splits[2], (LENGTH, KVH * HD), 1.0, 6.0, ((0, 64), (1, 4))),
        "segment_ids": jnp.searchsorted(jnp.cumsum(ragged(splits[3], DOCS, LENGTH, LENGTH // 2, 0)), jnp.arange(LENGTH), side="right").astype(jnp.int32),
        "cart_keys": draw_cart_keys(jax.random.fold_in(splits[6], 71), 0),
        "cart_values": noise(splits[5], (SLOTS, KVH * HD), 1.0, 6.0, ((0, 64), (1, 4))),
    }


distill_weight = 8.0

def rounded(array):
    return lax.optimization_barrier(array.astype(jnp.bfloat16)).astype(jnp.float32)

def reference(queries, keys, values, segment_ids, cart_keys, cart_values):
    group_size = HQ // KVH
    score_scale = 1.0 / math.sqrt(HD)
    slot_keys = cart_keys.astype(jnp.float32).reshape(SLOTS, KVH, HD)
    slot_values = cart_values.astype(jnp.float32).reshape(SLOTS, KVH, HD)
    positions = jnp.arange(LENGTH, dtype=jnp.int32)
    query_blocks = queries.astype(jnp.float32).reshape(N_CTX, TOK_DEV, KVH, group_size, HD)
    key_rows = keys.astype(jnp.float32).reshape(LENGTH, KVH, HD)
    value_rows = values.astype(jnp.float32).reshape(LENGTH, KVH, HD)
    segments = segment_ids

    def teach(inputs):
        query_block, query_pos, query_seg = inputs
        scores = jnp.einsum('ikgd,jkd->kgij', query_block, key_rows) * score_scale
        allowed = (positions[None, :] <= query_pos[:, None]) & (segments[None, :] == query_seg[:, None])
        scores = jnp.where(allowed[None, None], scores, -jnp.inf)
        top_score = lax.optimization_barrier(jnp.max(scores, axis=-1, keepdims=True))
        weights = jnp.exp(scores - top_score)
        total = lax.optimization_barrier(jnp.sum(weights, axis=-1, keepdims=True))
        mixed = jnp.einsum('kgij,jkd->kgid', rounded(weights), value_rows) / total
        return jnp.transpose(mixed, (2, 0, 1, 3)).reshape(TOK_DEV, HQ * HD).astype(jnp.bfloat16)
    teacher_blocks = lax.map(teach, (query_blocks, positions.reshape(N_CTX, TOK_DEV), segments.reshape(N_CTX, TOK_DEV)))

    def learn(carry, inputs):
        key_grad, value_grad = carry
        query_block, teacher_block = inputs
        target = teacher_block.astype(jnp.float32).reshape(TOK_DEV, KVH, group_size, HD)
        logits = jnp.einsum('ikgd,skd->kgis', query_block, slot_keys) * score_scale
        top_logit = lax.optimization_barrier(jnp.max(logits, axis=-1, keepdims=True))
        expo = jnp.exp(logits - top_logit)
        probs = expo / lax.optimization_barrier(jnp.sum(expo, axis=-1, keepdims=True))
        probs_low = rounded(probs)
        student = jnp.einsum('kgis,skd->ikgd', probs_low, slot_values)
        delta = rounded(distill_weight * (student - target))
        back = jnp.einsum('ikgd,skd->kgis', delta, slot_values)
        row_term = jnp.einsum('ikgd,ikgd->kgi', delta, student)[..., None]
        score_grad = rounded(probs * (back - row_term))
        value_grad = value_grad + jnp.einsum('kgis,ikgd->skd', probs_low, delta)
        key_grad = key_grad + score_scale * jnp.einsum('kgis,ikgd->skd', score_grad, query_block)
        return ((key_grad, value_grad), student.reshape(TOK_DEV, HQ * HD).astype(jnp.bfloat16))
    (key_grad_total, value_grad_total), student_blocks = lax.scan(learn, (jnp.zeros((SLOTS, KVH, HD), jnp.float32), jnp.zeros((SLOTS, KVH, HD), jnp.float32)), (query_blocks, teacher_blocks))
    teacher_out = teacher_blocks.reshape(LENGTH, HQ * HD)
    reordered = student_blocks.reshape(N_CTX, N_CTX, TOK_DEV // N_CTX, HQ * HD)
    student_out = jnp.transpose(reordered, (1, 0, 2, 3)).reshape(LENGTH, HQ * HD)
    return (teacher_out, student_out, key_grad_total.reshape(SLOTS, KVH * HD), value_grad_total.reshape(SLOTS, KVH * HD))
```

```python
import functools
import math

import jax
import jax.numpy as jnp
from jax import lax
from jax.experimental import pallas as pl
from jax.experimental.pallas import tpu as pltpu
from jax.sharding import PartitionSpec as P

HQ = 32
KVH = 4
HD = 128
NX, NY, NQ = 4, 2, 8
ROWS = 128
PAIRS = 4
WIDE = 256
F32, BF16 = jnp.float32, jnp.bfloat16
MESH = pl.DeviceIdType.MESH
MASKED = -1e30
WEIGHT = 8.0
SCALE = 1.0 / math.sqrt(HD)
EXP2_SCALE = SCALE * math.log2(math.e)


def dot_nn(a, b):
    return lax.dot_general(a, b, (((1,), (0,)), ((), ())), preferred_element_type=F32)


def dot_nt(a, b):
    return lax.dot_general(a, b, (((1,), (1,)), ((), ())), preferred_element_type=F32)


def kernel(
    NZ, NDP,
    q_ref, k_hbm, v_hbm, cart_hbm,
    t_out, s_out, gk_out, gv_out,
    kvbuf, cartbuf, qrows, vt, ck, cv, cvt, m_ref, l_ref, acc, p_ref, plow, ot_ref,
    sbuf, rbuf1, s2buf, rbuf2, gk_acc, gv_acc, gbuf, rs1, zbuf, rs2, fbuf, dbuf,
    loc_sem, send_sem, kvz_sem, kv_sem, cart_sem, cartz_sem, a1_sem, a2_sem, r1_sem, r2_sem, dp_sem,
):
    NP = min(5, NZ)
    me = lax.axis_index("ctx")
    d = lax.axis_index("dp")
    rem, div = lax.rem, lax.div
    z = div(me, NQ)
    q = rem(me, NQ)
    x = div(q, NY)
    y = rem(q, NY)
    xp, xm, xo, yo = rem(x + 1, NX), rem(x + 3, NX), rem(x + 2, NX), 1 - y
    zp, zm = rem(z + 1, NZ), rem(z + NZ - 1, NZ)

    def ctx(zz, qq):
        return zz * NQ + qq

    to_zp, to_zm = ctx(zp, q), ctx(zm, q)

    def qi(xx, yy):
        return xx * NY + yy

    sent = []

    def copy(src, dst, ssem, rsem, to, to_dp):
        return pltpu.make_async_remote_copy(
            src_ref=src, dst_ref=dst, send_sem=ssem, recv_sem=rsem,
            device_id=(to, to_dp), device_id_type=MESH,
        )

    def send(refs, to, to_dp=None, cond=None):
        slot = len(sent)

        def make():
            src, dst, rsem = refs()
            return copy(src, dst, send_sem.at[slot], rsem, to, d if to_dp is None else to_dp)

        sent.append((cond, make))
        make().start()

    def recv(dst, rsem):
        copy(dst, dst, send_sem.at[0], rsem, me, d).wait_recv()

    barrier = pltpu.get_barrier_semaphore()
    peers = 0
    for r in range(1, NQ):
        pl.semaphore_signal(barrier, 1, device_id=(ctx(z, rem(q + r, NQ)), d), device_id_type=MESH)
        peers += 1
    for r in range(1, NZ):
        pl.semaphore_signal(barrier, 1, device_id=(ctx(rem(z + r, NZ), q), d), device_id_type=MESH)
        peers += 1
    for r in range(1, NDP):
        pl.semaphore_signal(barrier, 1, device_id=(me, rem(d + r, NDP)), device_id_type=MESH)
        peers += 1

    own = [
        pltpu.make_async_copy(cart_hbm, cartbuf.at[z, q], loc_sem.at[0]),
        pltpu.make_async_copy(k_hbm, kvbuf.at[0, q, 0], loc_sem.at[1]),
        pltpu.make_async_copy(v_hbm, kvbuf.at[0, q, 1], loc_sem.at[2]),
    ]
    for c in own:
        c.start()
    for c in own:
        c.wait()
    pl.semaphore_wait(barrier, peers)

    def cart_start():
        for r in range(1, NQ):
            send(lambda: (cartbuf.at[z, q], cartbuf.at[z, q], cart_sem.at[q]), ctx(z, rem(q + r, NQ)))

    UP, DOWN = NZ // 2, NZ - 1 - NZ // 2

    def cart_hop(h):
        if h == 0:
            for r in range(1, NQ):
                s = rem(q + r, NQ)
                recv(cartbuf.at[z, s], cart_sem.at[s])
        elif h <= UP:
            s = rem(z + NZ - h, NZ)
            recv(cartbuf.at[s], cartz_sem.at[s])
        if h < UP:
            s = rem(z + NZ - h, NZ)
            send(lambda s=s: (cartbuf.at[s], cartbuf.at[s], cartz_sem.at[s]), to_zp)
        if 1 <= h <= DOWN:
            s = rem(z + h, NZ)
            recv(cartbuf.at[s], cartz_sem.at[s])
        if h < DOWN:
            s = rem(z + h, NZ)
            send(lambda s=s: (cartbuf.at[s], cartbuf.at[s], cartz_sem.at[s]), to_zm)

    def when(k, body):
        if k == 0:
            body(None)
        else:
            pl.when(z >= k)(lambda: body(k))

    def unit(k, qq, j):
        return kvbuf.at[k, qq, j]

    def half(k, qq, j, h):
        return kvbuf.at[k, qq, j, pl.ds(h * 64, 64)]

    def pass_on(k, cond, qq, j, to, h=None):
        if h is None:
            send(lambda: (unit(k, qq, j), unit(k, qq, j), kv_sem.at[k, qq, j, 0]), to, cond=cond)
        else:
            send(lambda: (half(k, qq, j, h), half(k, qq, j, h), kv_sem.at[k, qq, j, h]), to, cond=cond)

    def got(k, qq, j, h=None):
        if h is None:
            recv(unit(k, qq, j), kv_sem.at[k, qq, j, 0])
        else:
            recv(half(k, qq, j, h), kv_sem.at[k, qq, j, h])

    at = {(n, m): qi(xx, yy) for n, xx in (("0", x), ("-", xm), ("+", xp), ("o", xo)) for m, yy in ((0, y), (1, yo))}
    to_xp, to_xm, to_y = ctx(z, qi(xp, y)), ctx(z, qi(xm, y)), ctx(z, qi(x, yo))

    def z_step(k):
        if k > 0:
            @pl.when(z >= k)
            def _():
                recv(kvbuf.at[k, q], kvz_sem.at[k])
        if k + 1 < NP:
            slot_cond = ("z", k)
            @pl.when((z >= k) & (z < NZ - 1))
            def _():
                send(lambda: (kvbuf.at[k, q], kvbuf.at[k + 1, q], kvz_sem.at[k + 1]), to_zp, cond=slot_cond)

    def round0(k):
        def body(c):
            pass_on(k, c, q, 0, to_y)
            pass_on(k, c, q, 1, to_xp)
            pass_on(k, c, q, 1, to_xm)
            pass_on(k, c, q, 0, to_xp)
            pass_on(k, c, q, 0, to_xm)
            pass_on(k, c, q, 1, to_y)
        when(k, body)

    def round1(k):
        def body(c):
            s = at["0", 1]
            got(k, s, 0)
            pass_on(k, c, s, 0, to_xp)
            pass_on(k, c, s, 0, to_xm)
            sm, sp = at["-", 0], at["+", 0]
            got(k, sm, 1)
            pass_on(k, c, sm, 1, to_xp, 0)
            pass_on(k, c, sm, 1, to_y)
            got(k, sp, 1)
            pass_on(k, c, sp, 1, to_xm, 1)
            pass_on(k, c, sp, 1, to_y)
            got(k, sm, 0)
            pass_on(k, c, sm, 0, to_xp, 0)
            got(k, sp, 0)
            pass_on(k, c, sp, 0, to_xm, 1)
        when(k, body)

    def round2(k):
        def body(c):
            so = at["o", 0]
            got(k, so, 1, 0)
            got(k, so, 1, 1)
            pass_on(k, c, so, 1, to_y)
            sm, sp = at["-", 1], at["+", 1]
            got(k, sm, 0)
            pass_on(k, c, sm, 0, to_xp, 0)
            got(k, sp, 0)
            pass_on(k, c, sp, 0, to_xm, 1)
        when(k, body)

    def round3(k):
        def body(c):
            for m in (0, 1):
                got(k, at["o", m], 0, 0)
                got(k, at["o", m], 0, 1)
            for n in ("0", "-", "+", "o"):
                got(k, at[n, 1], 1)
        when(k, body)

    eye = (
        lax.broadcasted_iota(jnp.int32, (ROWS, ROWS), 0)
        == lax.broadcasted_iota(jnp.int32, (ROWS, ROWS), 1)
    ).astype(F32).astype(BF16)

    def swap_matrix():
        i = lax.broadcasted_iota(jnp.int32, (ROWS, ROWS), 0)
        j = lax.broadcasted_iota(jnp.int32, (ROWS, ROWS), 1)
        src = ((i >> 1) & 7) * 16 + (i >> 4) * 2 + (i & 1)
        return (src == j).astype(F32).astype(BF16)

    def prepare():
        for h in range(8):
            qrows[h * ROWS:(h + 1) * ROWS, :] = q_ref[:, h * HD:(h + 1) * HD]

    def teacher(k):
        def body(c):
            zk = rem(z + NZ - k, NZ)
            segs = cartbuf[zk, :, 32:48, :].astype(F32)
            own_seg = cartbuf[z, q, 32:48, :].astype(F32)[0:1, :]
            first = jnp.zeros((1, ROWS), F32)
            for s in (1, 2, 3):
                below = jnp.where(segs < s, 1.0, 0.0)
                below = jnp.sum(below, axis=0)
                below = jnp.sum(below, axis=0, keepdims=True)
                below = jnp.sum(below, axis=1, keepdims=True)
                first = jnp.where(own_seg == s, below, first)
            first = first.astype(jnp.int32)
            first = jnp.concatenate([first, first], axis=1)
            key_rows = kvbuf[k, :, 0].reshape(NQ * ROWS, HD)
            value_rows = kvbuf[k, :, 1].reshape(NQ * ROWS, HD)
            vt[...] = dot_nt(eye, value_rows).astype(BF16)
            last = q * ROWS + lax.broadcasted_iota(jnp.int32, (1, ROWS), 1)
            last = jnp.concatenate([last, last], axis=1)

            def pair(hp, carry):
                heads = qrows[pl.ds(pl.multiple_of(hp * WIDE, WIDE), WIDE), :]
                scores = dot_nt(key_rows, heads)
                pos = lax.broadcasted_iota(jnp.int32, scores.shape, 0)
                allowed = pos >= first
                if k == 0:
                    allowed = allowed & (pos <= last)
                scores = jnp.where(allowed, scores, MASKED)
                top = jnp.max(scores, axis=0, keepdims=True)
                if k > 0:
                    old = m_ref[hp]
                    top = jnp.maximum(top, old)
                    factor = jnp.exp2((old - top) * EXP2_SCALE)
                weights = jnp.exp2((scores - top) * EXP2_SCALE)
                total = jnp.sum(weights, axis=0, keepdims=True)
                mixed = dot_nn(vt[...], weights.astype(BF16))
                if k > 0:
                    total = total + l_ref[hp] * factor
                    mixed = mixed + acc[hp] * factor
                m_ref[hp] = top
                l_ref[hp] = total
                acc[hp] = mixed
                return carry

            lax.fori_loop(0, PAIRS, pair, 0)
        when(k, body)

    SL = NZ * NQ * 16

    def student():
        ck[...] = cartbuf[:, :, 0:16, :].reshape(SL, HD)
        cv[...] = cartbuf[:, :, 16:32, :].reshape(SL, HD)
        cvt[...] = dot_nt(eye, cv[...]).astype(BF16)
        swap = swap_matrix()

        for hp in range(PAIRS):
            heads = qrows[hp * WIDE:(hp + 1) * WIDE, :]
            logits = dot_nt(ck[...], heads)
            top = jnp.max(logits, axis=0, keepdims=True)
            expo = jnp.exp2((logits - top) * EXP2_SCALE)
            total = jnp.sum(expo, axis=0, keepdims=True)
            probs = expo * (1.0 / total)
            low = probs.astype(BF16)
            p_ref[hp] = probs
            plow[hp] = low
            out = dot_nn(cvt[...], low)
            ot_ref[hp] = out
            out_low = out.astype(BF16)
            for g in range(2):
                h = hp * 2 + g
                rows = dot_nt(swap, out_low[:, g * ROWS:(g + 1) * ROWS])
                sbuf[:, :, h * HD:(h + 1) * HD] = rows.astype(BF16).reshape(NQ, 16, HD)

    def exchange1():
        for r in range(1, NQ):
            t = rem(q + r, NQ)
            send(lambda t=t: (sbuf.at[t], rbuf1.at[q], a1_sem.at[q]), ctx(z, t))

    def exchange2():
        for r in range(1, NQ):
            s = rem(q + r, NQ)
            recv(rbuf1.at[s], a1_sem.at[s])
        rbuf1[q] = sbuf[q]
        swap = swap_matrix()
        s2buf[...] = dot_nn(swap, rbuf1[...].reshape(ROWS, 1024)).astype(BF16).reshape(NQ, 16, 1024)
        for r in range(1, NZ):
            t = rem(z + r, NZ)
            send(lambda t=t: (s2buf.at[t], rbuf2.at[z], a2_sem.at[z]), ctx(t, q))

    def exchange3():
        for r in range(1, NZ):
            s = rem(z + r, NZ)
            recv(rbuf2.at[s], a2_sem.at[s])
        rbuf2[z] = s2buf[z]
        s_out[...] = rbuf2[...].reshape(NZ * 16, 1024)

    def backward():
        for hp in range(PAIRS):
            low_t = (acc[hp] / l_ref[hp]).astype(BF16)
            out = ot_ref[hp]
            delta = (WEIGHT * (out - low_t.astype(F32))).astype(BF16)
            for g in range(2):
                h = hp * 2 + g
                t_out[:, h * HD:(h + 1) * HD] = dot_nt(eye, low_t[:, g * ROWS:(g + 1) * ROWS]).astype(BF16)
            row_term = jnp.sum(delta.astype(F32) * out, axis=0, keepdims=True)
            back = dot_nn(cv[...], delta)
            ds = (p_ref[hp] * (back - row_term)).astype(BF16)
            gv = dot_nt(plow[hp], delta)
            gk = dot_nn(ds, qrows[hp * WIDE:(hp + 1) * WIDE, :])
            if hp > 0:
                gv = gv + gv_acc[...]
                gk = gk + gk_acc[...]
            if hp < PAIRS - 1:
                gv_acc[...] = gv
                gk_acc[...] = gk
            else:
                gbuf[:, :, 0] = (gk * SCALE).astype(BF16).reshape(NZ, NQ, 16, HD)
                gbuf[:, :, 1] = gv.astype(BF16).reshape(NZ, NQ, 16, HD)

    def reduce1():
        for r in range(1, NQ):
            t = rem(q + r, NQ)
            send(lambda t=t: (gbuf.at[:, t], rs1.at[q], r1_sem.at[q]), ctx(z, t))

    def reduce2():
        total = gbuf[:, q].astype(F32)
        for r in range(1, NQ):
            s = rem(q + r, NQ)
            recv(rs1.at[s], r1_sem.at[s])
            total = total + rs1[s].astype(F32)
        zbuf[...] = total.astype(BF16)
        for r in range(1, NZ):
            t = rem(z + r, NZ)
            send(lambda t=t: (zbuf.at[t], rs2.at[z], r2_sem.at[z]), ctx(t, q))

    def reduce3():
        total = zbuf[z].astype(F32)
        for r in range(1, NZ):
            s = rem(z + r, NZ)
            recv(rs2.at[s], r2_sem.at[s])
            total = total + rs2[s].astype(F32)
        fbuf[...] = total
        for r in range(1, NDP):
            t = rem(d + r, NDP)
            send(lambda: (fbuf, dbuf.at[d], dp_sem.at[d]), me, to_dp=t)
        dbuf[d] = total

    def reduce4():
        for r in range(1, NDP):
            s = rem(d + r, NDP)
            recv(dbuf.at[s], dp_sem.at[s])
        for s in range(NDP):
            gk_out[:, s * HD:(s + 1) * HD] = dbuf[s, 0]
            gv_out[:, s * HD:(s + 1) * HD] = dbuf[s, 1]

    cart_start()
    z_step(0)
    round0(0)
    prepare()
    STEPS = NP + 3
    hops = max(UP, DOWN) + 1
    fed = max(hops, 5)
    for t in range(1, max(STEPS, fed + 2)):
        if t - 1 < hops:
            cart_hop(t - 1)
        if t < NP:
            z_step(t)
        for age, part in ((2, round2), (1, round1), (0, round0)):
            if 0 <= t - age < NP:
                part(t - age)
        if t == fed:
            student()
            exchange1()
        if 0 <= t - 3 < NP:
            round3(t - 3)
            teacher(t - 3)
        if t == fed + 1:
            exchange2()
    backward()
    reduce1()
    exchange3()
    reduce2()
    reduce3()
    reduce4()
    for cond, make in sent:
        if cond is None:
            make().wait_send()
        elif isinstance(cond, tuple):
            pl.when((z >= cond[1]) & (z < NZ - 1))(lambda: make().wait_send())
        else:
            pl.when(z >= cond)(lambda: make().wait_send())


def per_device(NZ, NDP, queries, keys, values, segment_ids, cart_keys, cart_values):
    NP = min(5, NZ)
    SL = NZ * NQ * 16
    seg = jnp.broadcast_to(segment_ids.astype(BF16)[None, :], (16, ROWS))
    seg = jnp.where(jnp.arange(16)[:, None] == 0, seg, jnp.bfloat16(100.0))
    cart = jnp.concatenate([cart_keys, cart_values, seg], axis=0)
    V = pltpu.VMEM
    D = pltpu.SemaphoreType.DMA
    vmem = pl.BlockSpec(memory_space=pltpu.VMEM)
    hbm = pl.BlockSpec(memory_space=pl.ANY)
    return pl.pallas_call(
        functools.partial(kernel, NZ, NDP),
        out_shape=[
            jax.ShapeDtypeStruct((ROWS, 1024), BF16),
            jax.ShapeDtypeStruct((NZ * 16, 1024), BF16),
            jax.ShapeDtypeStruct((16, NDP * HD), F32),
            jax.ShapeDtypeStruct((16, NDP * HD), F32),
        ],
        in_specs=[vmem, hbm, hbm, hbm],
        out_specs=[vmem] * 4,
        scratch_shapes=[
            V((NP, NQ, 2, ROWS, HD), BF16),
            V((NZ, NQ, 48, HD), BF16),
            V((1024, HD), BF16),
            V((HD, NQ * ROWS), BF16),
            V((SL, HD), BF16),
            V((SL, HD), BF16),
            V((HD, SL), BF16),
            V((PAIRS, 1, WIDE), F32),
            V((PAIRS, 1, WIDE), F32),
            V((PAIRS, HD, WIDE), F32),
            V((PAIRS, SL, WIDE), F32),
            V((PAIRS, SL, WIDE), BF16),
            V((PAIRS, HD, WIDE), F32),
            V((NQ, 16, 1024), BF16),
            V((NQ, 16, 1024), BF16),
            V((NQ, 16, 1024), BF16),
            V((NZ, 16, 1024), BF16),
            V((SL, HD), F32),
            V((SL, HD), F32),
            V((NZ, NQ, 2, 16, HD), BF16),
            V((NQ, NZ, 2, 16, HD), BF16),
            V((NZ, 2, 16, HD), BF16),
            V((NZ, 2, 16, HD), BF16),
            V((2, 16, HD), F32),
            V((NDP, 2, 16, HD), F32),
            D((3,)), D((160,)), D((NP,)), D((NP, NQ, 2, 2)), D((NQ,)), D((NZ,)),
            D((NQ,)), D((NZ,)), D((NQ,)), D((NZ,)), D((NDP,)),
        ],
        compiler_params=pltpu.CompilerParams(
            collective_id=0, has_side_effects=True, vmem_limit_bytes=60 * 1024 * 1024
        ),
        name="distill",
    )(queries, keys, values, cart)


def solution(mesh):
    nz, ndp = mesh.shape["ctx"] // NQ, mesh.shape["dp"]
    specs = (
        P("ctx", "dp"), P("ctx", "dp"), P("ctx", "dp"), P("ctx"), P("ctx", "dp"), P("ctx", "dp"),
    )
    return jax.shard_map(
        functools.partial(per_device, nz, ndp), mesh=mesh, in_specs=specs,
        out_specs=(P("ctx", "dp"), P("ctx", "dp"), P("ctx", None), P("ctx", None)),
        check_vma=False,
    )
```

```python
import functools
import math

import jax
import jax.numpy as jnp
from jax import lax
from jax.experimental import pallas as pl
from jax.experimental.pallas import tpu as pltpu
from jax.sharding import PartitionSpec as P

HQ = 32
KVH = 4
HD = 128
NX, NY, NQ = 4, 2, 8
ROWS = 128
PAIRS = 4
WIDE = 256
F32, BF16 = jnp.float32, jnp.bfloat16
MESH = pl.DeviceIdType.MESH
MASKED = -1e30
WEIGHT = 8.0
SCALE = 1.0 / math.sqrt(HD)
EXP2_SCALE = SCALE * math.log2(math.e)


def dot_nn(a, b):
    return lax.dot_general(a, b, (((1,), (0,)), ((), ())), preferred_element_type=F32)


def dot_nt(a, b):
    return lax.dot_general(a, b, (((1,), (1,)), ((), ())), preferred_element_type=F32)


def kernel(
    NZ, NDP,
    q_ref, k_hbm, v_hbm, seg_hbm, ck_hbm, cv_hbm,
    t_out, s_out, gk_out, gv_out,
    kvbuf, segbuf, cartbuf, qrows, vt, ck, cv, cvt, m_ref, l_ref, acc, p_ref, plow, ot_ref,
    delta_ref, row_ref, ds_ref,
    sbuf, rbuf1, s2buf, rbuf2, gbuf, rs1, zbuf, rs2, fbuf, dbuf,
    loc_sem, send_sem, kvz_sem, kv_sem, seg_sem, segz_sem, cart_sem, cartz_sem,
    a1_sem, a2_sem, r1_sem, r2_sem, dp_sem,
):
    NP = min(5, NZ)
    SL = NZ * NQ * 16
    rem, div = lax.rem, lax.div
    me = lax.axis_index("ctx")
    d = lax.axis_index("dp")
    z = div(me, NQ)
    q = rem(me, NQ)
    x = div(q, NY)
    y = rem(q, NY)

    def ctx(zz, qq):
        return rem(zz, NZ) * NQ + qq

    def at(dx, flip):
        return rem(x + dx, NX) * NY + (1 - y if flip else y)

    def guarded(cond, body):
        if cond is None:
            body()
        else:
            pl.when(cond())(body)

    sent = []

    def send(refs, to, cond=None):
        slot = len(sent)

        def make():
            src, dst, rsem = refs()
            place, part = to()
            return pltpu.make_async_remote_copy(
                src_ref=src, dst_ref=dst, send_sem=send_sem.at[slot], recv_sem=rsem,
                device_id=(place, part), device_id_type=MESH,
            )

        sent.append((cond, make))
        guarded(cond, lambda: make().start())

    def recv(refs, cond=None):
        def body():
            dst, rsem = refs()
            pltpu.make_async_remote_copy(
                src_ref=dst, dst_ref=dst, send_sem=send_sem.at[0], recv_sem=rsem,
                device_id=(me, d), device_id_type=MESH,
            ).wait_recv()

        guarded(cond, body)

    barrier = pltpu.get_barrier_semaphore()

    def greet():
        for r in range(1, NZ):
            pl.semaphore_signal(barrier, 1, device_id=(ctx(z + r, q), d), device_id_type=MESH)
        for r in range(1, NDP):
            pl.semaphore_signal(barrier, 1, device_id=(me, rem(d + r, NDP)), device_id_type=MESH)
        for r in range(1, NQ):
            pl.semaphore_signal(barrier, 1, device_id=(ctx(z, rem(q + r, NQ)), d), device_id_type=MESH)

    def own_copies():
        return [
            pltpu.make_async_copy(k_hbm, kvbuf.at[0, q, pl.ds(0, ROWS)], loc_sem.at[0]),
            pltpu.make_async_copy(v_hbm, kvbuf.at[0, q, pl.ds(ROWS, ROWS)], loc_sem.at[1]),
            pltpu.make_async_copy(seg_hbm, segbuf.at[0, q], loc_sem.at[2]),
            pltpu.make_async_copy(ck_hbm, cartbuf.at[z, q, 0], loc_sem.at[3]),
            pltpu.make_async_copy(cv_hbm, cartbuf.at[z, q, 1], loc_sem.at[4]),
        ]

    def seg_start():
        for r in range(1, NQ):
            send(lambda: (segbuf.at[0, q], segbuf.at[0, q], seg_sem.at[q]),
                 lambda r=r: (ctx(z, rem(q + r, NQ)), d))

    def seg_spread():
        for r in range(1, NQ):
            recv(lambda r=r: (segbuf.at[0, rem(q + r, NQ)], seg_sem.at[rem(q + r, NQ)]))
        for k in range(1, NP):
            send(lambda k=k: (segbuf.at[0], segbuf.at[k], segz_sem.at[k]),
                 lambda k=k: (ctx(z + k, q), d), lambda k=k: z + k < NZ)

    def seg_wait(k):
        if k > 0:
            recv(lambda: (segbuf.at[k], segz_sem.at[k]), lambda: z >= k)

    def plane(r):
        return rem(z + r + NZ, NZ)

    def cart_start():
        for r in range(1, NQ):
            send(lambda: (cartbuf.at[z, q], cartbuf.at[z, q], cart_sem.at[q]),
                 lambda r=r: (ctx(z, rem(q + r, NQ)), d))

    near = [r for r in ((1, -1, 2, -2) if NZ >= 8 else range(1, NZ))]

    def cart_spread():
        for r in range(1, NQ):
            recv(lambda r=r: (cartbuf.at[z, rem(q + r, NQ)], cart_sem.at[rem(q + r, NQ)]))
        for r in near:
            send(lambda: (cartbuf.at[z], cartbuf.at[z], cartz_sem.at[z, 0]),
                 lambda r=r: (ctx(z + r + NZ, q), d))

    def cart_relay():
        if NZ < 8:
            return
        for r in (-2, 2):
            part = 0 if r < 0 else 1
            step = 1 if r < 0 else -1
            recv(lambda r=r: (cartbuf.at[plane(r)], cartz_sem.at[plane(r), 0]))
            send(lambda r=r: (cartbuf.at[plane(r)], cartbuf.at[plane(r)], cartz_sem.at[plane(r), 0]),
                 lambda step=step: (ctx(z + step + NZ, q), d))
            send(lambda r=r, p=part: (cartbuf.at[plane(r), pl.ds(p * 4, 4)], cartbuf.at[plane(r), pl.ds(p * 4, 4)],
                                      cartz_sem.at[plane(r), p]),
                 lambda step=step: (ctx(z + 2 * step + NZ, q), d))

    def cart_wait():
        if NZ < 8:
            for r in near:
                recv(lambda r=r: (cartbuf.at[plane(-r)], cartz_sem.at[plane(-r), 0]))
            return
        for r in (-1, 1, -3, 3):
            recv(lambda r=r: (cartbuf.at[plane(r)], cartz_sem.at[plane(r), 0]))
        for p in (0, 1):
            recv(lambda p=p: (cartbuf.at[plane(4), pl.ds(p * 4, 4)], cartz_sem.at[plane(4), p]))

    CUT = 96
    LOW, HIGH = (0, CUT), (CUT, 2 * ROWS - CUT)

    def piece(k, qq, part):
        return kvbuf.at[k, qq, pl.ds(part[0], part[1])]

    def need(k, src, dst):
        if k == 0:
            return lambda: dst() > src()
        if k == 4:
            return lambda: (z >= 4) & (dst() < src())
        return lambda: z >= k

    def exists(k):
        return None if k == 0 else (lambda: z >= k)

    def hand(k, src, dst, part, cond):
        i = 0 if part is LOW else 1
        send(lambda: (piece(k, src(), part), piece(k, src(), part), kv_sem.at[k, src(), i]),
             lambda: (ctx(z, dst()), d), cond)

    def take(k, src, part, cond):
        i = 0 if part is LOW else 1
        recv(lambda: (piece(k, src(), part), kv_sem.at[k, src(), i]), cond)

    home = lambda: q
    twin = lambda: at(0, True)

    def z_send(k, steps):
        send(lambda: (kvbuf.at[k, q], kvbuf.at[k + steps, q], kvz_sem.at[k + steps]),
             lambda: (ctx(z + steps, q), d), lambda: (z >= k) & (z + steps < NZ))

    def z_recv(k):
        recv(lambda: (kvbuf.at[k, q], kvz_sem.at[k]), lambda: z >= k)
        if k == 2:
            for steps in (1, 2):
                if k + steps < NP:
                    z_send(k, steps)

    def round0(k):
        hand(k, home, twin, LOW, exists(k))
        for dx in (2, 1, 3):
            there = lambda dx=dx: at(dx, False)
            hand(k, home, there, HIGH, need(k, home, there))
        for dx in (2, 1, 3):
            there = lambda dx=dx: at(dx, False)
            hand(k, home, there, LOW, need(k, home, there))
        hand(k, home, twin, HIGH, need(k, home, twin))

    def round1(k):
        take(k, twin, LOW, exists(k))
        for dx in (2, 1, 3):
            there = lambda dx=dx: at(dx, False)
            hand(k, twin, there, LOW, need(k, twin, there))
        for dx in (1, 3, 2):
            source = lambda dx=dx: at(dx, False)
            take(k, source, HIGH, need(k, source, home))
            hand(k, source, twin, HIGH, need(k, source, twin))

    def round2(k):
        for dx in (1, 3, 2):
            for flip in (False, True):
                source = lambda dx=dx, flip=flip: at(dx, flip)
                take(k, source, LOW, need(k, source, home))
        for dx in (0, 1, 3, 2):
            source = lambda dx=dx: at(dx, True)
            take(k, source, HIGH, need(k, source, home))

    eye = (
        lax.broadcasted_iota(jnp.int32, (ROWS, ROWS), 0)
        == lax.broadcasted_iota(jnp.int32, (ROWS, ROWS), 1)
    ).astype(F32).astype(BF16)

    def swap_matrix():
        i = lax.broadcasted_iota(jnp.int32, (ROWS, ROWS), 0)
        j = lax.broadcasted_iota(jnp.int32, (ROWS, ROWS), 1)
        src = ((i >> 1) & 7) * 16 + (i >> 4) * 2 + (i & 1)
        return (src == j).astype(F32).astype(BF16)

    def prepare():
        for h in range(8):
            qrows[h * ROWS:(h + 1) * ROWS, :] = q_ref[:, h * HD:(h + 1) * HD]
        for s in range(NQ):
            @pl.when(s > q)
            def _():
                kvbuf[0, s, ROWS:2 * ROWS, :] = jnp.zeros((ROWS, HD), BF16)
            if NP == 5:
                @pl.when(s < q)
                def _():
                    kvbuf[4, s, ROWS:2 * ROWS, :] = jnp.zeros((ROWS, HD), BF16)

    def teacher(k, c0=0, count=NQ, cond=None):
        def body():
            segs = segbuf[k].reshape(NQ, ROWS)
            own_seg = segbuf[0, q]
            first = jnp.zeros((1, ROWS), F32)
            for s in (1, 2, 3):
                below = jnp.where(segs < s, 1.0, 0.0)
                below = jnp.sum(below, axis=0, keepdims=True)
                below = jnp.sum(below, axis=1, keepdims=True)
                first = jnp.where(own_seg == s, below, first)
            first = first.astype(jnp.int32) - c0 * ROWS
            first = jnp.concatenate([first, first], axis=1)
            key_rows = kvbuf[k, c0:c0 + count, 0:ROWS, :].reshape(count * ROWS, HD)
            value_rows = kvbuf[k, c0:c0 + count, ROWS:2 * ROWS, :].reshape(count * ROWS, HD)
            vt[:, :count * ROWS] = dot_nt(eye, value_rows).astype(BF16)
            last = (q - c0) * ROWS + lax.broadcasted_iota(jnp.int32, (1, ROWS), 1)
            last = jnp.concatenate([last, last], axis=1)
            opening = k == 0 and c0 == 0

            def pair(hp, carry):
                heads = qrows[pl.ds(pl.multiple_of(hp * WIDE, WIDE), WIDE), :]
                scores = dot_nt(key_rows, heads)
                pos = lax.broadcasted_iota(jnp.int32, scores.shape, 0)
                allowed = pos >= first
                if k == 0:
                    allowed = allowed & (pos <= last)
                scores = jnp.where(allowed, scores, MASKED)
                top = jnp.max(scores, axis=0, keepdims=True)
                if not opening:
                    old = m_ref[hp]
                    top = jnp.maximum(top, old)
                    factor = jnp.exp2((old - top) * EXP2_SCALE)
                weights = jnp.exp2((scores - top) * EXP2_SCALE)
                total = jnp.sum(weights, axis=0, keepdims=True)
                mixed = dot_nn(vt[:, :count * ROWS], weights.astype(BF16))
                if not opening:
                    total = total + l_ref[hp] * factor
                    mixed = mixed + acc[hp] * factor
                m_ref[hp] = top
                l_ref[hp] = total
                acc[hp] = mixed
                return carry

            lax.fori_loop(0, PAIRS, pair, 0)

        guarded(cond, body)

    def teach(k):
        seg_wait(k)
        if k == 0:
            teacher(0, 0, 4)
            teacher(0, 4, 4, lambda: q >= 4)
        elif k == 4:
            teacher(4, 4, 4, lambda: z >= 4)
            teacher(4, 0, 4, lambda: (z >= 4) & (q < 4))
        else:
            teacher(k, 0, NQ, lambda: z >= k)

    def student():
        ck[...] = cartbuf[:, :, 0].reshape(SL, HD)
        cv[...] = cartbuf[:, :, 1].reshape(SL, HD)
        cvt[...] = dot_nt(eye, cv[...]).astype(BF16)
        swap = swap_matrix()
        for hp in range(PAIRS):
            cols = slice(hp * WIDE, (hp + 1) * WIDE)
            logits = dot_nt(ck[...], qrows[cols, :])
            top = jnp.max(logits, axis=0, keepdims=True)
            expo = jnp.exp2((logits - top) * EXP2_SCALE)
            total = jnp.sum(expo, axis=0, keepdims=True)
            probs = expo * (1.0 / total)
            low = probs.astype(BF16)
            p_ref[:, cols] = probs
            plow[:, cols] = low
            out = dot_nn(cvt[...], low)
            ot_ref[:, cols] = out
            out_low = out.astype(BF16)
            for g in range(2):
                h = hp * 2 + g
                rows = dot_nt(swap, out_low[:, g * ROWS:(g + 1) * ROWS])
                sbuf[:, :, h * HD:(h + 1) * HD] = rows.astype(BF16).reshape(NQ, 16, HD)

    def exchange1():
        for r in range(1, NQ):
            send(lambda r=r: (sbuf.at[rem(q + r, NQ)], rbuf1.at[q], a1_sem.at[q]),
                 lambda r=r: (ctx(z, rem(q + r, NQ)), d))

    def exchange2():
        for r in range(1, NQ):
            recv(lambda r=r: (rbuf1.at[rem(q + r, NQ)], a1_sem.at[rem(q + r, NQ)]))
        rbuf1[q] = sbuf[q]
        swap = swap_matrix()
        s2buf[...] = dot_nn(swap, rbuf1[...].reshape(ROWS, 1024)).astype(BF16).reshape(NQ, 16, 1024)
        for r in range(1, NZ):
            send(lambda r=r: (s2buf.at[plane(r)], rbuf2.at[z], a2_sem.at[z]),
                 lambda r=r: (ctx(z + r, q), d))

    def exchange3():
        for r in range(1, NZ):
            recv(lambda r=r: (rbuf2.at[plane(r)], a2_sem.at[plane(r)]))
        rbuf2[z] = s2buf[z]
        s_out[...] = rbuf2[...].reshape(NZ * 16, 1024)

    def difference():
        for hp in range(PAIRS):
            cols = slice(hp * WIDE, (hp + 1) * WIDE)
            low_t = (acc[hp] / l_ref[hp]).astype(BF16)
            out = ot_ref[:, cols]
            delta = (WEIGHT * (out - low_t.astype(F32))).astype(BF16)
            delta_ref[:, cols] = delta
            row_ref[:, cols] = jnp.sum(delta.astype(F32) * out, axis=0, keepdims=True)
            for g in range(2):
                h = hp * 2 + g
                t_out[:, h * HD:(h + 1) * HD] = dot_nt(eye, low_t[:, g * ROWS:(g + 1) * ROWS]).astype(BF16)

    NH = 2
    HZ = NZ // NH

    def gradients(half):
        n = SL // NH
        rows = slice(half * n, (half + 1) * n)
        for hp in range(PAIRS):
            cols = slice(hp * WIDE, (hp + 1) * WIDE)
            back = dot_nn(cv[rows, :], delta_ref[:, cols])
            ds_ref[:, cols] = (p_ref[rows, cols] * (back - row_ref[:, cols])).astype(BF16)
        gv = dot_nt(plow[rows, :], delta_ref[...])
        gk = dot_nn(ds_ref[...], qrows[...])
        planes = slice(half * HZ, (half + 1) * HZ)
        gbuf[planes, :, 0] = (gk * SCALE).astype(BF16).reshape(HZ, NQ, 16, HD)
        gbuf[planes, :, 1] = gv.astype(BF16).reshape(HZ, NQ, 16, HD)

    def reduce1(half):
        planes = pl.ds(half * HZ, HZ)
        for r in range(1, NQ):
            send(lambda r=r: (gbuf.at[planes, rem(q + r, NQ)], rs1.at[q, planes], r1_sem.at[q, half]),
                 lambda r=r: (ctx(z, rem(q + r, NQ)), d))

    def reduce2(half):
        planes = pl.ds(half * HZ, HZ)
        total = gbuf[planes, q].astype(F32)
        for r in range(1, NQ):
            recv(lambda r=r: (rs1.at[rem(q + r, NQ), planes], r1_sem.at[rem(q + r, NQ), half]))
        for r in range(1, NQ):
            total = total + rs1[rem(q + r, NQ), planes].astype(F32)
        zbuf[planes] = total.astype(BF16)
        for t in range(half * HZ, (half + 1) * HZ):
            send(lambda t=t: (zbuf.at[t], rs2.at[z], r2_sem.at[z]),
                 lambda t=t: (ctx(t, q), d), lambda t=t: z != t)

    def reduce3():
        total = zbuf[z].astype(F32)
        for r in range(1, NZ):
            recv(lambda r=r: (rs2.at[plane(r)], r2_sem.at[plane(r)]))
        for r in range(1, NZ):
            total = total + rs2[plane(r)].astype(F32)
        fbuf[...] = total
        for r in range(1, NDP):
            send(lambda: (fbuf, dbuf.at[d], dp_sem.at[d]), lambda r=r: (me, rem(d + r, NDP)))
        dbuf[d] = total

    def reduce4():
        for r in range(1, NDP):
            recv(lambda r=r: (dbuf.at[rem(d + r, NDP)], dp_sem.at[rem(d + r, NDP)]))
        for s in range(NDP):
            gk_out[:, s * HD:(s + 1) * HD] = dbuf[s, 0]
            gv_out[:, s * HD:(s + 1) * HD] = dbuf[s, 1]

    def finish():
        for cond, make in sent:
            guarded(cond, lambda: make().wait_send())

    have = lambda k, part: part(k) if k < NP else None
    greet()
    own = own_copies()
    for c in own:
        c.start()
    prepare()
    for c in own:
        c.wait()
    pl.semaphore_wait(barrier, NQ - 1 + NZ - 1 + NDP - 1)
    z_send(0, 1)
    if NP > 2:
        z_send(0, 2)
    seg_start()
    cart_start()
    round0(0)
    seg_spread()
    cart_spread()
    have(1, z_recv)
    have(1, round0)
    round1(0)
    have(2, z_recv)
    have(2, round0)
    cart_relay()
    have(1, round1)
    have(3, z_recv)
    have(3, round0)
    round2(0)
    teach(0)
    have(2, round1)
    have(4, z_recv)
    have(4, round0)
    have(1, round2)
    have(1, teach)
    have(3, round1)
    cart_wait()
    student()
    have(4, round1)
    exchange1()
    for k in (2, 3, 4):
        have(k, round2)
        have(k, teach)
    exchange2()
    difference()
    gradients(0)
    reduce1(0)
    gradients(1)
    reduce1(1)
    reduce2(0)
    reduce2(1)
    reduce3()
    exchange3()
    reduce4()
    finish()


def write_out(t_ref, s_ref, gk_ref, gv_ref, t_hbm, s_hbm, gk_hbm, gv_hbm, sem):
    pairs = ((t_ref, t_hbm), (s_ref, s_hbm), (gk_ref, gk_hbm), (gv_ref, gv_hbm))
    copies = [pltpu.make_async_copy(a, b, sem.at[i]) for i, (a, b) in enumerate(pairs)]
    for c in copies:
        c.start()
    for c in copies:
        c.wait()


def per_device(NZ, NDP, queries, keys, values, segment_ids, cart_keys, cart_values):
    NP = min(5, NZ)
    SL = NZ * NQ * 16
    V = pltpu.VMEM
    D = pltpu.SemaphoreType.DMA
    vmem = pl.BlockSpec(memory_space=pltpu.VMEM)
    hbm = pl.BlockSpec(memory_space=pl.ANY)
    shapes = [
        jax.ShapeDtypeStruct((ROWS, 1024), BF16),
        jax.ShapeDtypeStruct((NZ * 16, 1024), BF16),
        jax.ShapeDtypeStruct((16, NDP * HD), F32),
        jax.ShapeDtypeStruct((16, NDP * HD), F32),
    ]
    results = pl.pallas_call(
        functools.partial(kernel, NZ, NDP),
        out_shape=shapes,
        in_specs=[vmem, hbm, hbm, hbm, hbm, hbm],
        out_specs=[vmem] * 4,
        scratch_shapes=[
            V((NP, NQ, 2 * ROWS, HD), BF16),
            V((NP, NQ, 1, ROWS), jnp.int32),
            V((NZ, NQ, 2, 16, HD), BF16),
            V((1024, HD), BF16),
            V((HD, NQ * ROWS), BF16),
            V((SL, HD), BF16),
            V((SL, HD), BF16),
            V((HD, SL), BF16),
            V((PAIRS, 1, WIDE), F32),
            V((PAIRS, 1, WIDE), F32),
            V((PAIRS, HD, WIDE), F32),
            V((SL, 1024), F32),
            V((SL, 1024), BF16),
            V((HD, 1024), F32),
            V((HD, 1024), BF16),
            V((1, 1024), F32),
            V((SL // 2, 1024), BF16),
            V((NQ, 16, 1024), BF16),
            V((NQ, 16, 1024), BF16),
            V((NQ, 16, 1024), BF16),
            V((NZ, 16, 1024), BF16),
            V((NZ, NQ, 2, 16, HD), BF16),
            V((NQ, NZ, 2, 16, HD), BF16),
            V((NZ, 2, 16, HD), BF16),
            V((NZ, 2, 16, HD), BF16),
            V((2, 16, HD), F32),
            V((NDP, 2, 16, HD), F32),
            D((5,)), D((160,)), D((NP,)), D((NP, NQ, 2)), D((NQ,)), D((NP,)), D((NQ,)), D((NZ, 2)),
            D((NQ,)), D((NZ,)), D((NQ, 2)), D((NZ,)), D((NDP,)),
        ],
        compiler_params=pltpu.CompilerParams(
            collective_id=0, has_side_effects=True, vmem_limit_bytes=60 * 1024 * 1024
        ),
        name="distill",
    )(queries, keys, values, segment_ids.reshape(1, ROWS), cart_keys, cart_values)
    return pl.pallas_call(
        write_out, out_shape=shapes, in_specs=[vmem] * 4, out_specs=[hbm] * 4,
        scratch_shapes=[D((4,))], name="write_out",
    )(*results)


def solution(mesh):
    nz, ndp = mesh.shape["ctx"] // NQ, mesh.shape["dp"]
    specs = (
        P("ctx", "dp"), P("ctx", "dp"), P("ctx", "dp"), P("ctx"), P("ctx", "dp"), P("ctx", "dp"),
    )
    return jax.shard_map(
        functools.partial(per_device, nz, ndp), mesh=mesh, in_specs=specs,
        out_specs=(P("ctx", "dp"), P("ctx", "dp"), P("ctx", None), P("ctx", None)),
        check_vma=False,
    )
```

```python
import functools
import math

import jax
import jax.numpy as jnp
from jax import lax
from jax.experimental import pallas as pl
from jax.experimental.pallas import tpu as pltpu
from jax.sharding import PartitionSpec as P

HQ = 32
KVH = 4
HD = 128
NX, NY, NQ = 4, 2, 8
ROWS = 128
PAIRS = 4
WIDE = 256
TILE = 256
F32, BF16 = jnp.float32, jnp.bfloat16
MESH = pl.DeviceIdType.MESH
MASKED = -1e30
WEIGHT = 8.0
SCALE = 1.0 / math.sqrt(HD)
EXP2_SCALE = SCALE * math.log2(math.e)


def dot_nn(a, b):
    return lax.dot_general(a, b, (((1,), (0,)), ((), ())), preferred_element_type=F32)


def dot_nt(a, b):
    return lax.dot_general(a, b, (((1,), (1,)), ((), ())), preferred_element_type=F32)


def kernel(
    NZ, NDP,
    q_ref, k_hbm, v_hbm, seg_hbm, ck_hbm, cv_hbm,
    t_out, s_out, gk_out, gv_out,
    kvbuf, segbuf, cartbuf, qrows, vt, ck, cv, cvt, m_ref, l_ref, acc, p_ref, plow, ot_ref,
    delta_ref, row_ref, ds_ref, s_ref,
    sbuf, rbuf1, s2buf, rbuf2, gbuf, rs1, zbuf, rs2, fbuf, dbuf,
    loc_sem, send_sem, kvz_sem, kv_sem, seg_sem, segz_sem, cart_sem, cartz_sem,
    a1_sem, a2_sem, r1_sem, r2_sem, dp_sem,
):
    NP = min(5, NZ)
    SL = NZ * NQ * 16
    rem, div = lax.rem, lax.div
    me = lax.axis_index("ctx")
    d = lax.axis_index("dp")
    z = div(me, NQ)
    q = rem(me, NQ)
    x = div(q, NY)
    y = rem(q, NY)

    def ctx(zz, qq):
        return rem(zz, NZ) * NQ + qq

    def at(dx, flip):
        return rem(x + dx, NX) * NY + (1 - y if flip else y)

    def guarded(cond, body):
        if cond is None:
            body()
        else:
            pl.when(cond())(body)

    sent = []

    def send(refs, to, cond=None):
        slot = len(sent)

        def make():
            src, dst, rsem = refs()
            place, part = to()
            return pltpu.make_async_remote_copy(
                src_ref=src, dst_ref=dst, send_sem=send_sem.at[slot], recv_sem=rsem,
                device_id=(place, part), device_id_type=MESH,
            )

        sent.append((cond, make))
        guarded(cond, lambda: make().start())

    def recv(refs, cond=None):
        def body():
            dst, rsem = refs()
            pltpu.make_async_remote_copy(
                src_ref=dst, dst_ref=dst, send_sem=send_sem.at[0], recv_sem=rsem,
                device_id=(me, d), device_id_type=MESH,
            ).wait_recv()

        guarded(cond, body)

    barrier = pltpu.get_barrier_semaphore()

    def greet():
        for r in range(1, NZ):
            pl.semaphore_signal(barrier, 1, device_id=(ctx(z + r, q), d), device_id_type=MESH)
        for r in range(1, NDP):
            pl.semaphore_signal(barrier, 1, device_id=(me, rem(d + r, NDP)), device_id_type=MESH)
        for r in range(1, NQ):
            pl.semaphore_signal(barrier, 1, device_id=(ctx(z, rem(q + r, NQ)), d), device_id_type=MESH)

    def own_copies():
        return [
            pltpu.make_async_copy(k_hbm, kvbuf.at[0, q, pl.ds(0, ROWS)], loc_sem.at[0]),
            pltpu.make_async_copy(v_hbm, kvbuf.at[0, q, pl.ds(ROWS, ROWS)], loc_sem.at[1]),
            pltpu.make_async_copy(seg_hbm, segbuf.at[0, q], loc_sem.at[2]),
            pltpu.make_async_copy(ck_hbm, cartbuf.at[z, q, 0], loc_sem.at[3]),
            pltpu.make_async_copy(cv_hbm, cartbuf.at[z, q, 1], loc_sem.at[4]),
        ]

    def seg_start():
        for r in range(1, NQ):
            send(lambda: (segbuf.at[0, q], segbuf.at[0, q], seg_sem.at[q]),
                 lambda r=r: (ctx(z, rem(q + r, NQ)), d))

    def seg_spread():
        for r in range(1, NQ):
            recv(lambda r=r: (segbuf.at[0, rem(q + r, NQ)], seg_sem.at[rem(q + r, NQ)]))
        for k in range(1, NP):
            send(lambda k=k: (segbuf.at[0], segbuf.at[k], segz_sem.at[k]),
                 lambda k=k: (ctx(z + k, q), d), lambda k=k: z + k < NZ)

    def seg_wait(k):
        if k > 0:
            recv(lambda: (segbuf.at[k], segz_sem.at[k]), lambda: z >= k)

    def plane(r):
        return rem(z + r + NZ, NZ)

    def cart_start():
        for r in range(1, NQ):
            send(lambda: (cartbuf.at[z, q], cartbuf.at[z, q], cart_sem.at[q]),
                 lambda r=r: (ctx(z, rem(q + r, NQ)), d))

    near = [r for r in ((1, -1, 2, -2) if NZ >= 8 else range(1, NZ))]

    def cart_spread():
        for r in range(1, NQ):
            recv(lambda r=r: (cartbuf.at[z, rem(q + r, NQ)], cart_sem.at[rem(q + r, NQ)]))
        for r in near:
            send(lambda: (cartbuf.at[z], cartbuf.at[z], cartz_sem.at[z, 0]),
                 lambda r=r: (ctx(z + r + NZ, q), d))

    def cart_relay():
        if NZ < 8:
            return
        for r in (-2, 2):
            part = 0 if r < 0 else 1
            step = 1 if r < 0 else -1
            recv(lambda r=r: (cartbuf.at[plane(r)], cartz_sem.at[plane(r), 0]))
            send(lambda r=r: (cartbuf.at[plane(r)], cartbuf.at[plane(r)], cartz_sem.at[plane(r), 0]),
                 lambda step=step: (ctx(z + step + NZ, q), d))
            send(lambda r=r, p=part: (cartbuf.at[plane(r), pl.ds(p * 4, 4)], cartbuf.at[plane(r), pl.ds(p * 4, 4)],
                                      cartz_sem.at[plane(r), p]),
                 lambda step=step: (ctx(z + 2 * step + NZ, q), d))

    def cart_wait():
        if NZ < 8:
            for r in near:
                recv(lambda r=r: (cartbuf.at[plane(-r)], cartz_sem.at[plane(-r), 0]))
            return
        for r in (-1, 1, -3, 3):
            recv(lambda r=r: (cartbuf.at[plane(r)], cartz_sem.at[plane(r), 0]))
        for p in (0, 1):
            recv(lambda p=p: (cartbuf.at[plane(4), pl.ds(p * 4, 4)], cartz_sem.at[plane(4), p]))

    CUT = 96
    LOW, HIGH = (0, CUT), (CUT, 2 * ROWS - CUT)

    def piece(k, qq, part):
        return kvbuf.at[k, qq, pl.ds(part[0], part[1])]

    def need(k, src, dst):
        if k == 0:
            return lambda: dst() > src()
        if k == 4:
            return lambda: (z >= 4) & (dst() < src())
        return lambda: z >= k

    def exists(k):
        return None if k == 0 else (lambda: z >= k)

    def hand(k, src, dst, part, cond):
        i = 0 if part is LOW else 1
        send(lambda: (piece(k, src(), part), piece(k, src(), part), kv_sem.at[k, src(), i]),
             lambda: (ctx(z, dst()), d), cond)

    def take(k, src, part, cond):
        i = 0 if part is LOW else 1
        recv(lambda: (piece(k, src(), part), kv_sem.at[k, src(), i]), cond)

    home = lambda: q
    twin = lambda: at(0, True)

    def z_send(k, steps):
        send(lambda: (kvbuf.at[k, q], kvbuf.at[k + steps, q], kvz_sem.at[k + steps]),
             lambda: (ctx(z + steps, q), d), lambda: (z >= k) & (z + steps < NZ))

    def z_recv(k):
        recv(lambda: (kvbuf.at[k, q], kvz_sem.at[k]), lambda: z >= k)
        if k == 2:
            for steps in (1, 2):
                if k + steps < NP:
                    z_send(k, steps)

    def round0(k):
        hand(k, home, twin, LOW, exists(k))
        for dx in (2, 1, 3):
            there = lambda dx=dx: at(dx, False)
            hand(k, home, there, HIGH, need(k, home, there))
        for dx in (2, 1, 3):
            there = lambda dx=dx: at(dx, False)
            hand(k, home, there, LOW, need(k, home, there))
        hand(k, home, twin, HIGH, need(k, home, twin))

    def round1(k):
        take(k, twin, LOW, exists(k))
        for dx in (2, 1, 3):
            there = lambda dx=dx: at(dx, False)
            hand(k, twin, there, LOW, need(k, twin, there))
        for dx in (1, 3, 2):
            source = lambda dx=dx: at(dx, False)
            take(k, source, HIGH, need(k, source, home))
            hand(k, source, twin, HIGH, need(k, source, twin))

    def round2(k):
        for dx in (1, 3, 2):
            for flip in (False, True):
                source = lambda dx=dx, flip=flip: at(dx, flip)
                take(k, source, LOW, need(k, source, home))
        for dx in (0, 1, 3, 2):
            source = lambda dx=dx: at(dx, True)
            take(k, source, HIGH, need(k, source, home))

    eye = (
        lax.broadcasted_iota(jnp.int32, (ROWS, ROWS), 0)
        == lax.broadcasted_iota(jnp.int32, (ROWS, ROWS), 1)
    ).astype(F32).astype(BF16)

    def swap_matrix():
        i = lax.broadcasted_iota(jnp.int32, (ROWS, ROWS), 0)
        j = lax.broadcasted_iota(jnp.int32, (ROWS, ROWS), 1)
        src = ((i >> 1) & 7) * 16 + (i >> 4) * 2 + (i & 1)
        return (src == j).astype(F32).astype(BF16)

    def prepare():
        for h in range(8):
            qrows[h * ROWS:(h + 1) * ROWS, :] = q_ref[:, h * HD:(h + 1) * HD]
        for s in range(NQ):
            @pl.when(s > q)
            def _():
                kvbuf[0, s, ROWS:2 * ROWS, :] = jnp.zeros((ROWS, HD), BF16)
            if NP == 5:
                @pl.when(s < q)
                def _():
                    kvbuf[4, s, ROWS:2 * ROWS, :] = jnp.zeros((ROWS, HD), BF16)

    def teacher(k, c0=0, count=NQ, cond=None):
        def body():
            segs = segbuf[k].reshape(NQ, ROWS)
            own_seg = segbuf[0, q]
            first = jnp.zeros((1, ROWS), F32)
            for s in (1, 2, 3):
                below = jnp.where(segs < s, 1.0, 0.0)
                below = jnp.sum(below, axis=0, keepdims=True)
                below = jnp.sum(below, axis=1, keepdims=True)
                first = jnp.where(own_seg == s, below, first)
            first = first.astype(jnp.int32) - c0 * ROWS
            first = jnp.concatenate([first, first], axis=1)
            key_rows = kvbuf[k, c0:c0 + count, 0:ROWS, :].reshape(count * ROWS, HD)
            value_rows = kvbuf[k, c0:c0 + count, ROWS:2 * ROWS, :].reshape(count * ROWS, HD)
            vt[:, :count * ROWS] = dot_nt(eye, value_rows).astype(BF16)
            last = (q - c0) * ROWS + lax.broadcasted_iota(jnp.int32, (1, ROWS), 1)
            last = jnp.concatenate([last, last], axis=1)
            opening = k == 0 and c0 == 0
            tiles = count * ROWS // TILE

            def scores(hp, j, top):
                part = dot_nt(key_rows[j * TILE:(j + 1) * TILE], qrows[hp * WIDE:(hp + 1) * WIDE, :])
                pos = lax.broadcasted_iota(jnp.int32, part.shape, 0) + j * TILE
                allowed = pos >= first
                if k == 0:
                    allowed = allowed & (pos <= last)
                part = jnp.where(allowed, part, MASKED)
                s_ref[hp % 2, j * TILE:(j + 1) * TILE, :] = part
                part = jnp.max(part.reshape(TILE // 8, 8, WIDE), axis=0)
                return part if top is None else jnp.maximum(top, part)

            top = None
            for j in range(tiles):
                top = scores(0, j, top)
            for hp in range(PAIRS):
                top = jnp.max(top, axis=0, keepdims=True)
                if not opening:
                    old = m_ref[hp]
                    top = jnp.maximum(top, old)
                    factor = jnp.exp2((old - top) * EXP2_SCALE)
                total, mixed, ahead = None, None, None
                for j in range(tiles):
                    rows = slice(j * TILE, (j + 1) * TILE)
                    weights = jnp.exp2((s_ref[hp % 2, rows, :] - top) * EXP2_SCALE)
                    if hp + 1 < PAIRS:
                        ahead = scores(hp + 1, j, ahead)
                    part = jnp.sum(weights.reshape(TILE // 8, 8, WIDE), axis=0)
                    total = part if total is None else total + part
                    part = dot_nn(vt[:, rows], weights.astype(BF16))
                    mixed = part if mixed is None else mixed + part
                total = jnp.sum(total, axis=0, keepdims=True)
                if not opening:
                    total = total + l_ref[hp] * factor
                    mixed = mixed + acc[hp] * factor
                m_ref[hp] = top
                l_ref[hp] = total
                acc[hp] = mixed
                top = ahead

        guarded(cond, body)

    def teach(k):
        seg_wait(k)
        if k == 0:
            teacher(0, 0, 4)
            teacher(0, 4, 4, lambda: q >= 4)
        elif k == 4:
            teacher(4, 4, 4, lambda: z >= 4)
            teacher(4, 0, 4, lambda: (z >= 4) & (q < 4))
        else:
            teacher(k, 0, NQ, lambda: z >= k)

    def student():
        ck[...] = cartbuf[:, :, 0].reshape(SL, HD)
        cv[...] = cartbuf[:, :, 1].reshape(SL, HD)
        cvt[...] = dot_nt(eye, cv[...]).astype(BF16)
        swap = swap_matrix()
        tiles = SL // TILE

        def logits(hp, j, top):
            part = dot_nt(ck[j * TILE:(j + 1) * TILE, :], qrows[hp * WIDE:(hp + 1) * WIDE, :])
            s_ref[hp % 2, j * TILE:(j + 1) * TILE, :] = part
            part = jnp.max(part.reshape(TILE // 8, 8, WIDE), axis=0)
            return part if top is None else jnp.maximum(top, part)

        def probabilities(hp, j, inverse, out):
            rows, cols = slice(j * TILE, (j + 1) * TILE), slice(hp * WIDE, (hp + 1) * WIDE)
            probs = p_ref[rows, cols] * inverse
            p_ref[rows, cols] = probs
            low = probs.astype(BF16)
            plow[rows, cols] = low
            part = dot_nn(cvt[:, rows], low)
            return part if out is None else out + part

        top, inverse = None, None
        for j in range(tiles):
            top = logits(0, j, top)
        for hp in range(PAIRS + 1):
            if hp < PAIRS:
                top = jnp.max(top, axis=0, keepdims=True)
            total, ahead, out = None, None, None
            for j in range(tiles):
                rows, cols = slice(j * TILE, (j + 1) * TILE), slice(hp * WIDE, (hp + 1) * WIDE)
                if hp < PAIRS:
                    expo = jnp.exp2((s_ref[hp % 2, rows, :] - top) * EXP2_SCALE)
                    p_ref[rows, cols] = expo
                    part = jnp.sum(expo.reshape(TILE // 8, 8, WIDE), axis=0)
                    total = part if total is None else total + part
                if hp + 1 < PAIRS:
                    ahead = logits(hp + 1, j, ahead)
                if hp > 0:
                    out = probabilities(hp - 1, j, inverse, out)
            if hp > 0:
                ot_ref[:, (hp - 1) * WIDE:hp * WIDE] = out
                out_low = out.astype(BF16)
                for g in range(2):
                    h = (hp - 1) * 2 + g
                    rows = dot_nt(swap, out_low[:, g * ROWS:(g + 1) * ROWS])
                    sbuf[:, :, h * HD:(h + 1) * HD] = rows.astype(BF16).reshape(NQ, 16, HD)
            if hp < PAIRS:
                inverse = 1.0 / jnp.sum(total, axis=0, keepdims=True)
            top = ahead

    def exchange1():
        for r in range(1, NQ):
            send(lambda r=r: (sbuf.at[rem(q + r, NQ)], rbuf1.at[q], a1_sem.at[q]),
                 lambda r=r: (ctx(z, rem(q + r, NQ)), d))

    def exchange2():
        for r in range(1, NQ):
            recv(lambda r=r: (rbuf1.at[rem(q + r, NQ)], a1_sem.at[rem(q + r, NQ)]))
        rbuf1[q] = sbuf[q]
        swap = swap_matrix()
        s2buf[...] = dot_nn(swap, rbuf1[...].reshape(ROWS, 1024)).astype(BF16).reshape(NQ, 16, 1024)
        for r in range(1, NZ):
            send(lambda r=r: (s2buf.at[plane(r)], rbuf2.at[z], a2_sem.at[z]),
                 lambda r=r: (ctx(z + r, q), d))

    def exchange3():
        for r in range(1, NZ):
            recv(lambda r=r: (rbuf2.at[plane(r)], a2_sem.at[plane(r)]))
        rbuf2[z] = s2buf[z]
        s_out[...] = rbuf2[...].reshape(NZ * 16, 1024)

    def difference():
        for hp in range(PAIRS):
            cols = slice(hp * WIDE, (hp + 1) * WIDE)
            low_t = (acc[hp] / l_ref[hp]).astype(BF16)
            out = ot_ref[:, cols]
            delta = (WEIGHT * (out - low_t.astype(F32))).astype(BF16)
            delta_ref[:, cols] = delta
            row_ref[:, cols] = jnp.sum(delta.astype(F32) * out, axis=0, keepdims=True)
            for g in range(2):
                h = hp * 2 + g
                t_out[:, h * HD:(h + 1) * HD] = dot_nt(eye, low_t[:, g * ROWS:(g + 1) * ROWS]).astype(BF16)

    NH = 2
    HZ = NZ // NH

    def gradients(half):
        n = SL // NH
        rows = slice(half * n, (half + 1) * n)
        for hp in range(PAIRS):
            cols = slice(hp * WIDE, (hp + 1) * WIDE)
            back = dot_nn(cv[rows, :], delta_ref[:, cols])
            ds_ref[:, cols] = (p_ref[rows, cols] * (back - row_ref[:, cols])).astype(BF16)
        gv = dot_nt(plow[rows, :], delta_ref[...])
        gk = dot_nn(ds_ref[...], qrows[...])
        planes = slice(half * HZ, (half + 1) * HZ)
        gbuf[planes, :, 0] = (gk * SCALE).astype(BF16).reshape(HZ, NQ, 16, HD)
        gbuf[planes, :, 1] = gv.astype(BF16).reshape(HZ, NQ, 16, HD)

    def reduce1(half):
        planes = pl.ds(half * HZ, HZ)
        for r in range(1, NQ):
            send(lambda r=r: (gbuf.at[planes, rem(q + r, NQ)], rs1.at[q, planes], r1_sem.at[q, half]),
                 lambda r=r: (ctx(z, rem(q + r, NQ)), d))

    def reduce2(half):
        planes = pl.ds(half * HZ, HZ)
        total = gbuf[planes, q].astype(F32)
        for r in range(1, NQ):
            recv(lambda r=r: (rs1.at[rem(q + r, NQ), planes], r1_sem.at[rem(q + r, NQ), half]))
        for r in range(1, NQ):
            total = total + rs1[rem(q + r, NQ), planes].astype(F32)
        zbuf[planes] = total.astype(BF16)
        for t in range(half * HZ, (half + 1) * HZ):
            send(lambda t=t: (zbuf.at[t], rs2.at[z], r2_sem.at[z]),
                 lambda t=t: (ctx(t, q), d), lambda t=t: z != t)

    def reduce3():
        total = zbuf[z].astype(F32)
        for r in range(1, NZ):
            recv(lambda r=r: (rs2.at[plane(r)], r2_sem.at[plane(r)]))
        for r in range(1, NZ):
            total = total + rs2[plane(r)].astype(F32)
        fbuf[...] = total
        for r in range(1, NDP):
            send(lambda: (fbuf, dbuf.at[d], dp_sem.at[d]), lambda r=r: (me, rem(d + r, NDP)))
        dbuf[d] = total

    def reduce4():
        for r in range(1, NDP):
            recv(lambda r=r: (dbuf.at[rem(d + r, NDP)], dp_sem.at[rem(d + r, NDP)]))
        for s in range(NDP):
            gk_out[:, s * HD:(s + 1) * HD] = dbuf[s, 0]
            gv_out[:, s * HD:(s + 1) * HD] = dbuf[s, 1]

    def finish():
        for cond, make in sent:
            guarded(cond, lambda: make().wait_send())

    have = lambda k, part: part(k) if k < NP else None
    greet()
    own = own_copies()
    for c in own:
        c.start()
    prepare()
    for c in own:
        c.wait()
    pl.semaphore_wait(barrier, NQ - 1 + NZ - 1 + NDP - 1)
    z_send(0, 1)
    if NP > 2:
        z_send(0, 2)
    seg_start()
    cart_start()
    round0(0)
    seg_spread()
    cart_spread()
    have(1, z_recv)
    have(1, round0)
    round1(0)
    have(2, z_recv)
    have(2, round0)
    cart_relay()
    have(1, round1)
    have(3, z_recv)
    have(3, round0)
    have(4, z_recv)
    have(4, round0)
    round2(0)
    teach(0)
    have(2, round1)
    have(1, round2)
    have(1, teach)
    have(3, round1)
    cart_wait()
    student()
    have(4, round1)
    exchange1()
    for k in (2, 3):
        have(k, round2)
        have(k, teach)
    have(4, round2)
    exchange2()
    have(4, teach)
    difference()
    gradients(0)
    reduce1(0)
    gradients(1)
    reduce1(1)
    reduce2(0)
    reduce2(1)
    reduce3()
    exchange3()
    reduce4()
    finish()


def write_out(t_ref, s_ref, gk_ref, gv_ref, t_hbm, s_hbm, gk_hbm, gv_hbm, sem):
    pairs = ((t_ref, t_hbm), (s_ref, s_hbm), (gk_ref, gk_hbm), (gv_ref, gv_hbm))
    copies = [pltpu.make_async_copy(a, b, sem.at[i]) for i, (a, b) in enumerate(pairs)]
    for c in copies:
        c.start()
    for c in copies:
        c.wait()


def per_device(NZ, NDP, queries, keys, values, segment_ids, cart_keys, cart_values):
    NP = min(5, NZ)
    SL = NZ * NQ * 16
    V = pltpu.VMEM
    D = pltpu.SemaphoreType.DMA
    vmem = pl.BlockSpec(memory_space=pltpu.VMEM)
    hbm = pl.BlockSpec(memory_space=pl.ANY)
    shapes = [
        jax.ShapeDtypeStruct((ROWS, 1024), BF16),
        jax.ShapeDtypeStruct((NZ * 16, 1024), BF16),
        jax.ShapeDtypeStruct((16, NDP * HD), F32),
        jax.ShapeDtypeStruct((16, NDP * HD), F32),
    ]
    results = pl.pallas_call(
        functools.partial(kernel, NZ, NDP),
        out_shape=shapes,
        in_specs=[vmem, hbm, hbm, hbm, hbm, hbm],
        out_specs=[vmem] * 4,
        scratch_shapes=[
            V((NP, NQ, 2 * ROWS, HD), BF16),
            V((NP, NQ, 1, ROWS), jnp.int32),
            V((NZ, NQ, 2, 16, HD), BF16),
            V((1024, HD), BF16),
            V((HD, NQ * ROWS), BF16),
            V((SL, HD), BF16),
            V((SL, HD), BF16),
            V((HD, SL), BF16),
            V((PAIRS, 1, WIDE), F32),
            V((PAIRS, 1, WIDE), F32),
            V((PAIRS, HD, WIDE), F32),
            V((SL, 1024), F32),
            V((SL, 1024), BF16),
            V((HD, 1024), F32),
            V((HD, 1024), BF16),
            V((1, 1024), F32),
            V((SL // 2, 1024), BF16),
            V((2, NQ * ROWS, WIDE), F32),
            V((NQ, 16, 1024), BF16),
            V((NQ, 16, 1024), BF16),
            V((NQ, 16, 1024), BF16),
            V((NZ, 16, 1024), BF16),
            V((NZ, NQ, 2, 16, HD), BF16),
            V((NQ, NZ, 2, 16, HD), BF16),
            V((NZ, 2, 16, HD), BF16),
            V((NZ, 2, 16, HD), BF16),
            V((2, 16, HD), F32),
            V((NDP, 2, 16, HD), F32),
            D((5,)), D((160,)), D((NP,)), D((NP, NQ, 2)), D((NQ,)), D((NP,)), D((NQ,)), D((NZ, 2)),
            D((NQ,)), D((NZ,)), D((NQ, 2)), D((NZ,)), D((NDP,)),
        ],
        compiler_params=pltpu.CompilerParams(
            collective_id=0, has_side_effects=True, vmem_limit_bytes=60 * 1024 * 1024
        ),
        name="distill",
    )(queries, keys, values, segment_ids.reshape(1, ROWS), cart_keys, cart_values)
    return pl.pallas_call(
        write_out, out_shape=shapes, in_specs=[vmem] * 4, out_specs=[hbm] * 4,
        scratch_shapes=[D((4,))], name="write_out",
    )(*results)


def solution(mesh):
    nz, ndp = mesh.shape["ctx"] // NQ, mesh.shape["dp"]
    specs = (
        P("ctx", "dp"), P("ctx", "dp"), P("ctx", "dp"), P("ctx"), P("ctx", "dp"), P("ctx", "dp"),
    )
    return jax.shard_map(
        functools.partial(per_device, nz, ndp), mesh=mesh, in_specs=specs,
        out_specs=(P("ctx", "dp"), P("ctx", "dp"), P("ctx", None), P("ctx", None)),
        check_vma=False,
    )
```

```python
import functools
import math

import jax
import jax.numpy as jnp
from jax import lax
from jax.experimental import pallas as pl
from jax.experimental.pallas import tpu as pltpu
from jax.sharding import PartitionSpec as P

HQ = 32
KVH = 4
HD = 128
NX, NY, NQ = 4, 2, 8
ROWS = 128
PAIRS = 4
WIDE = 256
TILE = 256
F32, BF16 = jnp.float32, jnp.bfloat16
MESH = pl.DeviceIdType.MESH
MASKED = -1e30
WEIGHT = 8.0
SCALE = 1.0 / math.sqrt(HD)
EXP2_SCALE = SCALE * math.log2(math.e)


def dot_nn(a, b):
    return lax.dot_general(a, b, (((1,), (0,)), ((), ())), preferred_element_type=F32)


def dot_nt(a, b):
    return lax.dot_general(a, b, (((1,), (1,)), ((), ())), preferred_element_type=F32)


def kernel(
    NZ, NDP,
    q_hbm, k_hbm, v_hbm, seg_hbm, ck_hbm, cv_hbm,
    t_out, s_out, gk_out, gv_out,
    kvbuf, segbuf, cartbuf, qrows, vt, ck, cv, cvt, m_ref, l_ref, acc, p_ref, plow, ot_ref,
    delta_ref, row_ref, ds_ref, s_ref, low_ref,
    sbuf, rbuf1, s2buf, rbuf2, gbuf, rs1, zbuf, rs2, fbuf, dbuf,
    loc_sem, send_sem, kvz_sem, kv_sem, seg_sem, segz_sem, cart_sem, cartz_sem,
    a1_sem, a2_sem, r1_sem, r2_sem, dp_sem,
):
    NP = min(5, NZ)
    SL = NZ * NQ * 16
    rem, div = lax.rem, lax.div
    me = lax.axis_index("ctx")
    d = lax.axis_index("dp")
    z = div(me, NQ)
    q = rem(me, NQ)
    x = div(q, NY)
    y = rem(q, NY)

    def ctx(zz, qq):
        return rem(zz, NZ) * NQ + qq

    def at(dx, flip):
        return rem(x + dx, NX) * NY + (1 - y if flip else y)

    def guarded(cond, body):
        if cond is None:
            body()
        else:
            pl.when(cond())(body)

    sent = []
    done = [0]

    def send(refs, to, cond=None):
        slot = len(sent)

        def make():
            src, dst, rsem = refs()
            place, part = to()
            return pltpu.make_async_remote_copy(
                src_ref=src, dst_ref=dst, send_sem=send_sem.at[slot], recv_sem=rsem,
                device_id=(place, part), device_id_type=MESH,
            )

        sent.append((cond, make))
        guarded(cond, lambda: make().start())

    def recv(refs, cond=None):
        def body():
            dst, rsem = refs()
            pltpu.make_async_remote_copy(
                src_ref=dst, dst_ref=dst, send_sem=send_sem.at[0], recv_sem=rsem,
                device_id=(me, d), device_id_type=MESH,
            ).wait_recv()

        guarded(cond, body)

    near = [r for r in ((1, -1, 2, -2) if NZ >= 8 else range(1, NZ))]

    barrier = pltpu.get_barrier_semaphore()

    def greet():
        for r in range(1, NZ):
            pl.semaphore_signal(barrier, 1, device_id=(ctx(z + r + NZ, q), d), device_id_type=MESH)
        for r in range(1, NDP):
            pl.semaphore_signal(barrier, 1, device_id=(me, rem(d + r, NDP)), device_id_type=MESH)
        for r in range(1, NQ):
            pl.semaphore_signal(barrier, 1, device_id=(ctx(z, rem(q + r, NQ)), d), device_id_type=MESH)

    def own_copies():
        return [
            pltpu.make_async_copy(k_hbm, kvbuf.at[0, q, pl.ds(0, ROWS)], loc_sem.at[0]),
            pltpu.make_async_copy(v_hbm, kvbuf.at[0, q, pl.ds(ROWS, ROWS)], loc_sem.at[1]),
            pltpu.make_async_copy(seg_hbm, segbuf.at[0, q], loc_sem.at[2]),
            pltpu.make_async_copy(ck_hbm, cartbuf.at[z, q, 0], loc_sem.at[3]),
            pltpu.make_async_copy(cv_hbm, cartbuf.at[z, q, 1], loc_sem.at[4]),
        ]

    def query_copies():
        return [
            pltpu.make_async_copy(q_hbm.at[:, pl.ds(h * HD, HD)], qrows.at[pl.ds(h * ROWS, ROWS)], loc_sem.at[5 + h])
            for h in range(8)
        ]

    def seg_start():
        for r in range(1, NQ):
            send(lambda: (segbuf.at[0, q], segbuf.at[0, q], seg_sem.at[q]),
                 lambda r=r: (ctx(z, rem(q + r, NQ)), d))

    def seg_spread():
        for r in range(1, NQ):
            recv(lambda r=r: (segbuf.at[0, rem(q + r, NQ)], seg_sem.at[rem(q + r, NQ)]))
        for k in range(1, min(NP, 3)):
            send(lambda k=k: (segbuf.at[0], segbuf.at[k], segz_sem.at[k]),
                 lambda k=k: (ctx(z + k, q), d), lambda k=k: z + k < NZ)

    def seg_relay():
        recv(lambda: (segbuf.at[2], segz_sem.at[2]), lambda: z >= 2)
        for k in range(3, NP):
            send(lambda k=k: (segbuf.at[2], segbuf.at[k], segz_sem.at[k]),
                 lambda k=k: (ctx(z + k - 2, q), d), lambda k=k: (z >= 2) & (z + k - 2 < NZ))

    def seg_wait(k):
        if k > 0 and k != 2:
            recv(lambda: (segbuf.at[k], segz_sem.at[k]), lambda: z >= k)

    def plane(r):
        return rem(z + r + NZ, NZ)

    def cart_start():
        for r in range(1, NQ):
            send(lambda: (cartbuf.at[z, q], cartbuf.at[z, q], cart_sem.at[q]),
                 lambda r=r: (ctx(z, rem(q + r, NQ)), d))


    def cart_spread():
        for r in range(1, NQ):
            recv(lambda r=r: (cartbuf.at[z, rem(q + r, NQ)], cart_sem.at[rem(q + r, NQ)]))
        for r in near:
            send(lambda: (cartbuf.at[z], cartbuf.at[z], cartz_sem.at[z, 0]),
                 lambda r=r: (ctx(z + r + NZ, q), d))

    def cart_relay():
        if NZ < 8:
            return
        for r in (-2, 2):
            part = 0 if r < 0 else 1
            step = 1 if r < 0 else -1
            recv(lambda r=r: (cartbuf.at[plane(r)], cartz_sem.at[plane(r), 0]))
            send(lambda r=r: (cartbuf.at[plane(r)], cartbuf.at[plane(r)], cartz_sem.at[plane(r), 0]),
                 lambda step=step: (ctx(z + step + NZ, q), d))
            send(lambda r=r, p=part: (cartbuf.at[plane(r), pl.ds(p * 4, 4)], cartbuf.at[plane(r), pl.ds(p * 4, 4)],
                                      cartz_sem.at[plane(r), p]),
                 lambda step=step: (ctx(z + 2 * step + NZ, q), d))

    def cart_wait():
        if NZ < 8:
            for r in near:
                recv(lambda r=r: (cartbuf.at[plane(-r)], cartz_sem.at[plane(-r), 0]))
            return
        for r in (-1, 1, -3, 3):
            recv(lambda r=r: (cartbuf.at[plane(r)], cartz_sem.at[plane(r), 0]))
        for p in (0, 1):
            recv(lambda p=p: (cartbuf.at[plane(4), pl.ds(p * 4, 4)], cartz_sem.at[plane(4), p]))

    CUT = 96
    LOW, HIGH, ALL = (0, CUT), (CUT, 2 * ROWS - CUT), (0, 2 * ROWS)

    def piece(k, qq, part):
        return kvbuf.at[k, qq, pl.ds(part[0], part[1])]

    def need(k, src, dst):
        if k == 0:
            return lambda: dst() > src()
        if k == 4:
            return lambda: (z >= 4) & (dst() < src())
        return lambda: z >= k

    def exists(k):
        return None if k == 0 else (lambda: z >= k)

    def hand(k, src, dst, part, cond):
        i = 1 if part is HIGH else 0
        send(lambda: (piece(k, src(), part), piece(k, src(), part), kv_sem.at[k, src(), i]),
             lambda: (ctx(z, dst()), d), cond)

    def take(k, src, part, cond):
        i = 1 if part is HIGH else 0
        recv(lambda: (piece(k, src(), part), kv_sem.at[k, src(), i]), cond)

    home = lambda: q
    twin = lambda: at(0, True)

    def z_send(k, steps):
        send(lambda: (kvbuf.at[k, q], kvbuf.at[k + steps, q], kvz_sem.at[k + steps]),
             lambda: (ctx(z + steps, q), d), lambda: (z >= k) & (z + steps < NZ))

    def z_recv(k):
        recv(lambda: (kvbuf.at[k, q], kvz_sem.at[k]), lambda: z >= k)
        if k == 2:
            for steps in (1,):
                if k + steps < NP:
                    z_send(k, steps)

    def direct(k):
        for dx, flip in ((2, True), (2, False), (1, True), (3, True), (1, False), (3, False), (0, True)):
            there = lambda dx=dx, flip=flip: at(dx, flip)
            hand(k, home, there, ALL, need(k, home, there))

    def direct_wait(k):
        for dx, flip in ((0, True), (1, False), (3, False), (1, True), (3, True), (2, False), (2, True)):
            source = lambda dx=dx, flip=flip: at(dx, flip)
            take(k, source, ALL, need(k, source, home))

    def round0(k):
        if k == 4:
            return direct(k)
        hand(k, home, twin, LOW, exists(k))
        for dx in (2, 1, 3):
            there = lambda dx=dx: at(dx, False)
            hand(k, home, there, HIGH, need(k, home, there))
        for dx in (2, 1, 3):
            there = lambda dx=dx: at(dx, False)
            hand(k, home, there, LOW, need(k, home, there))
        hand(k, home, twin, HIGH, need(k, home, twin))

    def round1(k):
        if k == 4:
            return
        take(k, twin, LOW, exists(k))
        for dx in (2, 1, 3):
            there = lambda dx=dx: at(dx, False)
            hand(k, twin, there, LOW, need(k, twin, there))
        for dx in (1, 3, 2):
            source = lambda dx=dx: at(dx, False)
            take(k, source, HIGH, need(k, source, home))
            hand(k, source, twin, HIGH, need(k, source, twin))

    def round2(k):
        if k == 4:
            return direct_wait(k)
        for dx in (1, 3, 2):
            for flip in (False, True):
                source = lambda dx=dx, flip=flip: at(dx, flip)
                take(k, source, LOW, need(k, source, home))
        for dx in (0, 1, 3, 2):
            source = lambda dx=dx: at(dx, True)
            take(k, source, HIGH, need(k, source, home))

    eye = (
        lax.broadcasted_iota(jnp.int32, (ROWS, ROWS), 0)
        == lax.broadcasted_iota(jnp.int32, (ROWS, ROWS), 1)
    ).astype(F32).astype(BF16)

    def swap_matrix():
        i = lax.broadcasted_iota(jnp.int32, (ROWS, ROWS), 0)
        j = lax.broadcasted_iota(jnp.int32, (ROWS, ROWS), 1)
        src = ((i >> 1) & 7) * 16 + (i >> 4) * 2 + (i & 1)
        return (src == j).astype(F32).astype(BF16)

    def prepare():
        for s in range(NQ):
            @pl.when(s > q)
            def _():
                kvbuf[0, s, ROWS:2 * ROWS, :] = jnp.zeros((ROWS, HD), BF16)
            if NP == 5:
                @pl.when(s < q)
                def _():
                    kvbuf[4, s, ROWS:2 * ROWS, :] = jnp.zeros((ROWS, HD), BF16)

    def teacher(k, c0=0, count=NQ, cond=None):
        def body():
            segs = segbuf[k].reshape(NQ, ROWS)
            own_seg = segbuf[0, q]
            first = jnp.zeros((1, ROWS), F32)
            for s in (1, 2, 3):
                below = jnp.where(segs < s, 1.0, 0.0)
                below = jnp.sum(below, axis=0, keepdims=True)
                below = jnp.sum(below, axis=1, keepdims=True)
                first = jnp.where(own_seg == s, below, first)
            first = first.astype(jnp.int32) - c0 * ROWS
            first = jnp.concatenate([first, first], axis=1)
            key_rows = kvbuf[k, c0:c0 + count, 0:ROWS, :].reshape(count * ROWS, HD)
            value_rows = kvbuf[k, c0:c0 + count, ROWS:2 * ROWS, :].reshape(count * ROWS, HD)
            vt[:, :count * ROWS] = dot_nt(eye, value_rows).astype(BF16)
            last = (q - c0) * ROWS + lax.broadcasted_iota(jnp.int32, (1, ROWS), 1)
            last = jnp.concatenate([last, last], axis=1)
            opening = k == 0 and c0 == 0
            tiles = count * ROWS // TILE

            def scores(hp, j, top):
                part = dot_nt(key_rows[j * TILE:(j + 1) * TILE], qrows[hp * WIDE:(hp + 1) * WIDE, :])
                pos = lax.broadcasted_iota(jnp.int32, part.shape, 0) + j * TILE
                allowed = pos >= first
                if k == 0:
                    allowed = allowed & (pos <= last)
                part = jnp.where(allowed, part, MASKED)
                s_ref[hp % 2, j * TILE:(j + 1) * TILE, :] = part
                part = jnp.max(part.reshape(TILE // 8, 8, WIDE), axis=0)
                return part if top is None else jnp.maximum(top, part)

            top = None
            for j in range(tiles):
                top = scores(0, j, top)
            for hp in range(PAIRS):
                top = jnp.max(top, axis=0, keepdims=True)
                if not opening:
                    old = m_ref[hp]
                    top = jnp.maximum(top, old)
                    factor = jnp.exp2((old - top) * EXP2_SCALE)
                total, mixed, ahead = None, None, None
                for j in range(tiles):
                    rows = slice(j * TILE, (j + 1) * TILE)
                    weights = jnp.exp2((s_ref[hp % 2, rows, :] - top) * EXP2_SCALE)
                    if hp + 1 < PAIRS:
                        ahead = scores(hp + 1, j, ahead)
                    part = jnp.sum(weights.reshape(TILE // 8, 8, WIDE), axis=0)
                    total = part if total is None else total + part
                    part = dot_nn(vt[:, rows], weights.astype(BF16))
                    mixed = part if mixed is None else mixed + part
                total = jnp.sum(total, axis=0, keepdims=True)
                if not opening:
                    total = total + l_ref[hp] * factor
                    mixed = mixed + acc[hp] * factor
                m_ref[hp] = top
                l_ref[hp] = total
                acc[hp] = mixed
                top = ahead

        guarded(cond, body)

    def teach(k):
        seg_wait(k)
        if k == 0:
            teacher(0, 0, 4)
            teacher(0, 4, 4, lambda: q >= 4)
        elif k == 4:
            teacher(4, 4, 4, lambda: z >= 4)
            teacher(4, 0, 4, lambda: (z >= 4) & (q < 4))
        else:
            teacher(k, 0, NQ, lambda: z >= k)

    def student():
        ck[...] = cartbuf[:, :, 0].reshape(SL, HD)
        cv[...] = cartbuf[:, :, 1].reshape(SL, HD)
        cvt[...] = dot_nt(eye, cv[...]).astype(BF16)
        swap = swap_matrix()
        tiles = SL // TILE

        def logits(hp, j, top):
            part = dot_nt(ck[j * TILE:(j + 1) * TILE, :], qrows[hp * WIDE:(hp + 1) * WIDE, :])
            s_ref[hp % 2, j * TILE:(j + 1) * TILE, :] = part
            part = jnp.max(part.reshape(TILE // 8, 8, WIDE), axis=0)
            return part if top is None else jnp.maximum(top, part)

        def probabilities(hp, j, inverse, out):
            rows, cols = slice(j * TILE, (j + 1) * TILE), slice(hp * WIDE, (hp + 1) * WIDE)
            probs = p_ref[rows, cols] * inverse
            p_ref[rows, cols] = probs
            low = probs.astype(BF16)
            plow[rows, cols] = low
            part = dot_nn(cvt[:, rows], low)
            return part if out is None else out + part

        top, inverse = None, None
        for j in range(tiles):
            top = logits(0, j, top)
        for hp in range(PAIRS + 1):
            if hp < PAIRS:
                top = jnp.max(top, axis=0, keepdims=True)
            total, ahead, out = None, None, None
            for j in range(tiles):
                rows, cols = slice(j * TILE, (j + 1) * TILE), slice(hp * WIDE, (hp + 1) * WIDE)
                if hp < PAIRS:
                    expo = jnp.exp2((s_ref[hp % 2, rows, :] - top) * EXP2_SCALE)
                    p_ref[rows, cols] = expo
                    part = jnp.sum(expo.reshape(TILE // 8, 8, WIDE), axis=0)
                    total = part if total is None else total + part
                if hp + 1 < PAIRS:
                    ahead = logits(hp + 1, j, ahead)
                if hp > 0:
                    out = probabilities(hp - 1, j, inverse, out)
            if hp > 0:
                ot_ref[:, (hp - 1) * WIDE:hp * WIDE] = out
                out_low = out.astype(BF16)
                for g in range(2):
                    h = (hp - 1) * 2 + g
                    rows = dot_nt(swap, out_low[:, g * ROWS:(g + 1) * ROWS])
                    sbuf[:, :, h * HD:(h + 1) * HD] = rows.astype(BF16).reshape(NQ, 16, HD)
            if hp < PAIRS:
                inverse = 1.0 / jnp.sum(total, axis=0, keepdims=True)
            top = ahead

    def exchange1():
        for r in range(1, NQ):
            send(lambda r=r: (sbuf.at[rem(q + r, NQ)], rbuf1.at[q], a1_sem.at[q]),
                 lambda r=r: (ctx(z, rem(q + r, NQ)), d))

    def exchange2():
        for r in range(1, NQ):
            recv(lambda r=r: (rbuf1.at[rem(q + r, NQ)], a1_sem.at[rem(q + r, NQ)]))
        rbuf1[q] = sbuf[q]
        swap = swap_matrix()
        s2buf[...] = dot_nn(swap, rbuf1[...].reshape(ROWS, 1024)).astype(BF16).reshape(NQ, 16, 1024)
        for r in range(1, NZ):
            send(lambda r=r: (s2buf.at[plane(r)], rbuf2.at[z], a2_sem.at[z]),
                 lambda r=r: (ctx(z + r, q), d))

    def exchange3():
        for r in range(1, NZ):
            recv(lambda r=r: (rbuf2.at[plane(r)], a2_sem.at[plane(r)]))
        rbuf2[z] = s2buf[z]
        s_out[...] = rbuf2[...].reshape(NZ * 16, 1024)

    def difference():
        for hp in range(PAIRS):
            cols = slice(hp * WIDE, (hp + 1) * WIDE)
            low_t = (acc[hp] / l_ref[hp]).astype(BF16)
            out = ot_ref[:, cols]
            delta = (WEIGHT * (out - low_t.astype(F32))).astype(BF16)
            delta_ref[:, cols] = delta
            row_ref[:, cols] = jnp.sum(delta.astype(F32) * out, axis=0, keepdims=True)
            low_ref[:, cols] = low_t

    def teacher_rows():
        for h in range(8):
            t_out[:, h * HD:(h + 1) * HD] = dot_nt(eye, low_ref[:, h * ROWS:(h + 1) * ROWS]).astype(BF16)

    NH = 2
    HZ = NZ // NH

    def gradients(half):
        n = SL // NH
        rows = slice(half * n, (half + 1) * n)
        for hp in range(PAIRS):
            cols = slice(hp * WIDE, (hp + 1) * WIDE)
            back = dot_nn(cv[rows, :], delta_ref[:, cols])
            ds_ref[:, cols] = (p_ref[rows, cols] * (back - row_ref[:, cols])).astype(BF16)
        gv = dot_nt(plow[rows, :], delta_ref[...])
        gk = dot_nn(ds_ref[...], qrows[...])
        planes = slice(half * HZ, (half + 1) * HZ)
        gbuf[planes, :, 0] = (gk * SCALE).astype(BF16).reshape(HZ, NQ, 16, HD)
        gbuf[planes, :, 1] = gv.astype(BF16).reshape(HZ, NQ, 16, HD)

    def reduce1(half):
        planes = pl.ds(half * HZ, HZ)
        for r in range(1, NQ):
            send(lambda r=r: (gbuf.at[planes, rem(q + r, NQ)], rs1.at[q, planes], r1_sem.at[q, half]),
                 lambda r=r: (ctx(z, rem(q + r, NQ)), d))

    def reduce2(half):
        planes = pl.ds(half * HZ, HZ)
        total = gbuf[planes, q].astype(F32)
        for r in range(1, NQ):
            recv(lambda r=r: (rs1.at[rem(q + r, NQ), planes], r1_sem.at[rem(q + r, NQ), half]))
        for r in range(1, NQ):
            total = total + rs1[rem(q + r, NQ), planes].astype(F32)
        zbuf[planes] = total.astype(BF16)
        for t in range(half * HZ, (half + 1) * HZ):
            send(lambda t=t: (zbuf.at[t], rs2.at[z], r2_sem.at[z]),
                 lambda t=t: (ctx(t, q), d), lambda t=t: z != t)

    def reduce3():
        total = zbuf[z].astype(F32)
        for r in range(1, NZ):
            recv(lambda r=r: (rs2.at[plane(r)], r2_sem.at[plane(r)]))
        for r in range(1, NZ):
            total = total + rs2[plane(r)].astype(F32)
        fbuf[...] = total
        for r in range(1, NDP):
            send(lambda: (fbuf, dbuf.at[d], dp_sem.at[d]), lambda r=r: (me, rem(d + r, NDP)))
        dbuf[d] = total

    def reduce4():
        for r in range(1, NDP):
            recv(lambda r=r: (dbuf.at[rem(d + r, NDP)], dp_sem.at[rem(d + r, NDP)]))
        for s in range(NDP):
            gk_out[:, s * HD:(s + 1) * HD] = dbuf[s, 0]
            gv_out[:, s * HD:(s + 1) * HD] = dbuf[s, 1]

    def finish(upto=None):
        upto = len(sent) if upto is None else upto
        for cond, make in sent[done[0]:upto]:
            guarded(cond, lambda: make().wait_send())
        done[0] = upto

    have = lambda k, part: part(k) if k < NP else None
    greet()
    own = own_copies()
    for c in own:
        c.start()
    asked = query_copies()
    for c in asked:
        c.start()
    prepare()
    for c in own:
        c.wait()
    pl.semaphore_wait(barrier, NQ - 1 + NZ - 1 + NDP - 1)
    for steps in (1, 2, 4):
        if steps < NP:
            z_send(0, steps)
    seg_start()
    cart_start()
    round0(0)
    for c in asked:
        c.wait()
    seg_spread()
    have(1, z_recv)
    have(1, round0)
    have(2, z_recv)
    have(2, round0)
    cart_spread()
    round1(0)
    if NP > 2:
        seg_relay()
    have(1, round1)
    have(3, z_recv)
    have(3, round0)
    have(4, z_recv)
    have(4, round0)
    round2(0)
    teach(0)
    have(2, round1)
    cart_relay()
    have(1, round2)
    have(1, teach)
    have(3, round1)
    cart_wait()
    student()
    exchange1()
    for k in (2, 3, 4):
        have(k, round2)
        have(k, teach)
    early = len(sent)
    difference()
    gradients(0)
    reduce1(0)
    gradients(1)
    reduce1(1)
    exchange2()
    teacher_rows()
    finish(early)
    reduce2(0)
    reduce2(1)
    reduce3()
    exchange3()
    reduce4()
    finish()


def write_out(t_ref, s_ref, gk_ref, gv_ref, t_hbm, s_hbm, gk_hbm, gv_hbm, sem):
    pairs = ((t_ref, t_hbm), (s_ref, s_hbm), (gk_ref, gk_hbm), (gv_ref, gv_hbm))
    copies = [pltpu.make_async_copy(a, b, sem.at[i]) for i, (a, b) in enumerate(pairs)]
    for c in copies:
        c.start()
    for c in copies:
        c.wait()


def per_device(NZ, NDP, queries, keys, values, segment_ids, cart_keys, cart_values):
    NP = min(5, NZ)
    SL = NZ * NQ * 16
    V = pltpu.VMEM
    D = pltpu.SemaphoreType.DMA
    vmem = pl.BlockSpec(memory_space=pltpu.VMEM)
    hbm = pl.BlockSpec(memory_space=pl.ANY)
    shapes = [
        jax.ShapeDtypeStruct((ROWS, 1024), BF16),
        jax.ShapeDtypeStruct((NZ * 16, 1024), BF16),
        jax.ShapeDtypeStruct((16, NDP * HD), F32),
        jax.ShapeDtypeStruct((16, NDP * HD), F32),
    ]
    results = pl.pallas_call(
        functools.partial(kernel, NZ, NDP),
        out_shape=[pltpu.VMEM(a.shape, a.dtype) for a in shapes],
        in_specs=[hbm] * 6,
        out_specs=[vmem] * 4,
        scratch_shapes=[
            V((NP, NQ, 2 * ROWS, HD), BF16),
            V((NP, NQ, 1, ROWS), jnp.int32),
            V((NZ, NQ, 2, 16, HD), BF16),
            V((1024, HD), BF16),
            V((HD, NQ * ROWS), BF16),
            V((SL, HD), BF16),
            V((SL, HD), BF16),
            V((HD, SL), BF16),
            V((PAIRS, 1, WIDE), F32),
            V((PAIRS, 1, WIDE), F32),
            V((PAIRS, HD, WIDE), F32),
            V((SL, 1024), F32),
            V((SL, 1024), BF16),
            V((HD, 1024), F32),
            V((HD, 1024), BF16),
            V((1, 1024), F32),
            V((SL // 2, 1024), BF16),
            V((2, NQ * ROWS, WIDE), F32),
            V((HD, 1024), BF16),
            V((NQ, 16, 1024), BF16),
            V((NQ, 16, 1024), BF16),
            V((NQ, 16, 1024), BF16),
            V((NZ, 16, 1024), BF16),
            V((NZ, NQ, 2, 16, HD), BF16),
            V((NQ, NZ, 2, 16, HD), BF16),
            V((NZ, 2, 16, HD), BF16),
            V((NZ, 2, 16, HD), BF16),
            V((2, 16, HD), F32),
            V((NDP, 2, 16, HD), F32),
            D((13,)), D((160,)), D((NP,)), D((NP, NQ, 2)), D((NQ,)), D((NP,)), D((NQ,)), D((NZ, 2)),
            D((NQ,)), D((NZ,)), D((NQ, 2)), D((NZ,)), D((NDP,)),
        ],
        compiler_params=pltpu.CompilerParams(
            collective_id=0, has_side_effects=True, vmem_limit_bytes=60 * 1024 * 1024
        ),
        name="distill",
    )(queries, keys, values, segment_ids.reshape(1, ROWS), cart_keys, cart_values)
    results = [pltpu.with_memory_space_constraint(a, pltpu.VMEM) for a in results]
    return pl.pallas_call(
        write_out, out_shape=shapes, in_specs=[vmem] * 4, out_specs=[hbm] * 4,
        scratch_shapes=[D((4,))], name="write_out",
    )(*results)


def solution(mesh):
    nz, ndp = mesh.shape["ctx"] // NQ, mesh.shape["dp"]
    specs = (
        P("ctx", "dp"), P("ctx", "dp"), P("ctx", "dp"), P("ctx"), P("ctx", "dp"), P("ctx", "dp"),
    )
    return jax.shard_map(
        functools.partial(per_device, nz, ndp), mesh=mesh, in_specs=specs,
        out_specs=(P("ctx", "dp"), P("ctx", "dp"), P("ctx", None), P("ctx", None)),
        check_vma=False,
    )
```

```python
import functools
import math

import jax
import jax.numpy as jnp
from jax import lax
from jax.experimental import pallas as pl
from jax.experimental.pallas import tpu as pltpu
from jax.sharding import PartitionSpec as P

HQ = 32
KVH = 4
HD = 128
NX, NY, NQ = 4, 2, 8
ROWS = 128
PAIRS = 4
WIDE = 256
TILE = 256
F32, BF16 = jnp.float32, jnp.bfloat16
MESH = pl.DeviceIdType.MESH
MASKED = -1e30
WEIGHT = 8.0
SCALE = 1.0 / math.sqrt(HD)
EXP2_SCALE = SCALE * math.log2(math.e)


def dot_nn(a, b):
    return lax.dot_general(a, b, (((1,), (0,)), ((), ())), preferred_element_type=F32)


def dot_nt(a, b):
    return lax.dot_general(a, b, (((1,), (1,)), ((), ())), preferred_element_type=F32)


def kernel(
    NZ, NDP,
    q_hbm, k_hbm, v_hbm, seg_hbm, ck_hbm, cv_hbm,
    t_out, s_out, gk_out, gv_out,
    kvbuf, segbuf, cartbuf, qrows, vt, ck, cv, cvt, m_ref, l_ref, acc, p_ref, plow, ot_ref,
    delta_ref, row_ref, ds_ref, s_ref, low_ref,
    sbuf, rbuf1, s2buf, rbuf2, gbuf, rs1, zbuf, rs2, fbuf, dbuf,
    loc_sem, send_sem, kvz_sem, kv_sem, seg_sem, segz_sem, cart_sem, cartz_sem,
    a1_sem, a2_sem, r1_sem, r2_sem, dp_sem,
):
    NP = min(5, NZ)
    SL = NZ * NQ * 16
    rem, div = lax.rem, lax.div
    me = lax.axis_index("ctx")
    d = lax.axis_index("dp")
    z = div(me, NQ)
    q = rem(me, NQ)
    x = div(q, NY)
    y = rem(q, NY)

    def ctx(zz, qq):
        return rem(zz, NZ) * NQ + qq

    def at(dx, flip):
        return rem(x + dx, NX) * NY + (1 - y if flip else y)

    def guarded(cond, body):
        if cond is None:
            body()
        else:
            pl.when(cond())(body)

    sent = []
    done = [0]

    def send(refs, to, cond=None):
        slot = len(sent)

        def make():
            src, dst, rsem = refs()
            place, part = to()
            return pltpu.make_async_remote_copy(
                src_ref=src, dst_ref=dst, send_sem=send_sem.at[slot], recv_sem=rsem,
                device_id=(place, part), device_id_type=MESH,
            )

        sent.append((cond, make))
        guarded(cond, lambda: make().start())

    def recv(refs, cond=None):
        def body():
            dst, rsem = refs()
            pltpu.make_async_remote_copy(
                src_ref=dst, dst_ref=dst, send_sem=send_sem.at[0], recv_sem=rsem,
                device_id=(me, d), device_id_type=MESH,
            ).wait_recv()

        guarded(cond, body)

    near = [r for r in ((1, -1, 2, -2) if NZ >= 8 else range(1, NZ))]

    barrier = pltpu.get_barrier_semaphore()

    def greet():
        for r in near:
            pl.semaphore_signal(barrier, 1, device_id=(ctx(z + r + NZ, q), d), device_id_type=MESH)
        for r in range(1, NDP):
            pl.semaphore_signal(barrier, 1, device_id=(me, rem(d + r, NDP)), device_id_type=MESH)
        for r in range(1, NQ):
            pl.semaphore_signal(barrier, 1, device_id=(ctx(z, rem(q + r, NQ)), d), device_id_type=MESH)

    def own_copies():
        return [
            pltpu.make_async_copy(k_hbm, kvbuf.at[0, q, pl.ds(0, ROWS)], loc_sem.at[0]),
            pltpu.make_async_copy(v_hbm, kvbuf.at[0, q, pl.ds(ROWS, ROWS)], loc_sem.at[1]),
            pltpu.make_async_copy(seg_hbm, segbuf.at[0, q], loc_sem.at[2]),
            pltpu.make_async_copy(ck_hbm, cartbuf.at[z, q, 0], loc_sem.at[3]),
            pltpu.make_async_copy(cv_hbm, cartbuf.at[z, q, 1], loc_sem.at[4]),
        ]

    def query_copies():
        return [
            pltpu.make_async_copy(q_hbm.at[:, pl.ds(h * HD, HD)], qrows.at[pl.ds(h * ROWS, ROWS)], loc_sem.at[5 + h])
            for h in range(8)
        ]

    def seg_start():
        for r in range(1, NQ):
            send(lambda: (segbuf.at[0, q], segbuf.at[0, q], seg_sem.at[q]),
                 lambda r=r: (ctx(z, rem(q + r, NQ)), d))

    def seg_spread():
        for r in range(1, NQ):
            recv(lambda r=r: (segbuf.at[0, rem(q + r, NQ)], seg_sem.at[rem(q + r, NQ)]))
        for k in range(1, min(NP, 3)):
            send(lambda k=k: (segbuf.at[0], segbuf.at[k], segz_sem.at[k]),
                 lambda k=k: (ctx(z + k, q), d), lambda k=k: z + k < NZ)

    def seg_relay():
        recv(lambda: (segbuf.at[2], segz_sem.at[2]), lambda: z >= 2)
        for k in range(3, NP):
            send(lambda k=k: (segbuf.at[2], segbuf.at[k], segz_sem.at[k]),
                 lambda k=k: (ctx(z + k - 2, q), d), lambda k=k: (z >= 2) & (z + k - 2 < NZ))

    def seg_wait(k):
        if k > 0 and k != 2:
            recv(lambda: (segbuf.at[k], segz_sem.at[k]), lambda: z >= k)

    def plane(r):
        return rem(z + r + NZ, NZ)

    def cart_start():
        for r in range(1, NQ):
            send(lambda: (cartbuf.at[z, q], cartbuf.at[z, q], cart_sem.at[q]),
                 lambda r=r: (ctx(z, rem(q + r, NQ)), d))


    def cart_spread():
        for r in range(1, NQ):
            recv(lambda r=r: (cartbuf.at[z, rem(q + r, NQ)], cart_sem.at[rem(q + r, NQ)]))
        for r in near:
            send(lambda: (cartbuf.at[z], cartbuf.at[z], cartz_sem.at[z, 0]),
                 lambda r=r: (ctx(z + r + NZ, q), d))

    def cart_relay():
        if NZ < 8:
            return
        for r in (-2, 2):
            part = 0 if r < 0 else 1
            step = 1 if r < 0 else -1
            recv(lambda r=r: (cartbuf.at[plane(r)], cartz_sem.at[plane(r), 0]))
            send(lambda r=r: (cartbuf.at[plane(r)], cartbuf.at[plane(r)], cartz_sem.at[plane(r), 0]),
                 lambda step=step: (ctx(z + step + NZ, q), d))
            send(lambda r=r, p=part: (cartbuf.at[plane(r), pl.ds(p * 4, 4)], cartbuf.at[plane(r), pl.ds(p * 4, 4)],
                                      cartz_sem.at[plane(r), p]),
                 lambda step=step: (ctx(z + 2 * step + NZ, q), d))

    def cart_wait():
        if NZ < 8:
            for r in near:
                recv(lambda r=r: (cartbuf.at[plane(-r)], cartz_sem.at[plane(-r), 0]))
            return
        for r in (-1, 1, -3, 3):
            recv(lambda r=r: (cartbuf.at[plane(r)], cartz_sem.at[plane(r), 0]))
        for p in (0, 1):
            recv(lambda p=p: (cartbuf.at[plane(4), pl.ds(p * 4, 4)], cartz_sem.at[plane(4), p]))

    CUT = 96
    LOW, HIGH, ALL = (0, CUT), (CUT, 2 * ROWS - CUT), (0, 2 * ROWS)

    def piece(k, qq, part):
        return kvbuf.at[k, qq, pl.ds(part[0], part[1])]

    def need(k, src, dst):
        if k == 0:
            return lambda: dst() > src()
        if k == 4:
            return lambda: (z >= 4) & (dst() < src())
        return lambda: z >= k

    def exists(k):
        return None if k == 0 else (lambda: z >= k)

    def hand(k, src, dst, part, cond):
        i = 1 if part is HIGH else 0
        send(lambda: (piece(k, src(), part), piece(k, src(), part), kv_sem.at[k, src(), i]),
             lambda: (ctx(z, dst()), d), cond)

    def take(k, src, part, cond):
        i = 1 if part is HIGH else 0
        recv(lambda: (piece(k, src(), part), kv_sem.at[k, src(), i]), cond)

    home = lambda: q
    twin = lambda: at(0, True)

    def z_send(k, steps):
        send(lambda: (kvbuf.at[k, q], kvbuf.at[k + steps, q], kvz_sem.at[k + steps]),
             lambda: (ctx(z + steps, q), d), lambda: (z >= k) & (z + steps < NZ))

    def z_recv(k):
        recv(lambda: (kvbuf.at[k, q], kvz_sem.at[k]), lambda: z >= k)
        if k == 2:
            for steps in (1, 2):
                if k + steps < NP:
                    z_send(k, steps)

    def direct(k):
        for dx, flip in ((2, True), (2, False), (1, True), (3, True), (1, False), (3, False), (0, True)):
            there = lambda dx=dx, flip=flip: at(dx, flip)
            hand(k, home, there, ALL, need(k, home, there))

    def direct_wait(k):
        for dx, flip in ((0, True), (1, False), (3, False), (1, True), (3, True), (2, False), (2, True)):
            source = lambda dx=dx, flip=flip: at(dx, flip)
            take(k, source, ALL, need(k, source, home))

    def round0(k):
        if k == 4:
            return direct(k)
        hand(k, home, twin, LOW, exists(k))
        for dx in (2, 1, 3):
            there = lambda dx=dx: at(dx, False)
            hand(k, home, there, HIGH, need(k, home, there))
        for dx in (2, 1, 3):
            there = lambda dx=dx: at(dx, False)
            hand(k, home, there, LOW, need(k, home, there))
        hand(k, home, twin, HIGH, need(k, home, twin))

    def round1(k):
        if k == 4:
            return
        take(k, twin, LOW, exists(k))
        for dx in (2, 1, 3):
            there = lambda dx=dx: at(dx, False)
            hand(k, twin, there, LOW, need(k, twin, there))
        for dx in (1, 3, 2):
            source = lambda dx=dx: at(dx, False)
            take(k, source, HIGH, need(k, source, home))
            hand(k, source, twin, HIGH, need(k, source, twin))

    def round2(k):
        if k == 4:
            return direct_wait(k)
        for dx in (1, 3, 2):
            for flip in (False, True):
                source = lambda dx=dx, flip=flip: at(dx, flip)
                take(k, source, LOW, need(k, source, home))
        for dx in (0, 1, 3, 2):
            source = lambda dx=dx: at(dx, True)
            take(k, source, HIGH, need(k, source, home))

    eye = (
        lax.broadcasted_iota(jnp.int32, (ROWS, ROWS), 0)
        == lax.broadcasted_iota(jnp.int32, (ROWS, ROWS), 1)
    ).astype(F32).astype(BF16)

    def swap_matrix():
        i = lax.broadcasted_iota(jnp.int32, (ROWS, ROWS), 0)
        j = lax.broadcasted_iota(jnp.int32, (ROWS, ROWS), 1)
        src = ((i >> 1) & 7) * 16 + (i >> 4) * 2 + (i & 1)
        return (src == j).astype(F32).astype(BF16)

    def prepare():
        for s in range(NQ):
            @pl.when(s > q)
            def _():
                kvbuf[0, s, ROWS:2 * ROWS, :] = jnp.zeros((ROWS, HD), BF16)
            if NP == 5:
                @pl.when(s < q)
                def _():
                    kvbuf[4, s, ROWS:2 * ROWS, :] = jnp.zeros((ROWS, HD), BF16)

    def teacher(k, c0=0, count=NQ, cond=None):
        def body():
            segs = segbuf[k].reshape(NQ, ROWS)
            own_seg = segbuf[0, q]
            first = jnp.zeros((1, ROWS), F32)
            for s in (1, 2, 3):
                below = jnp.where(segs < s, 1.0, 0.0)
                below = jnp.sum(below, axis=0, keepdims=True)
                below = jnp.sum(below, axis=1, keepdims=True)
                first = jnp.where(own_seg == s, below, first)
            first = first.astype(jnp.int32) - c0 * ROWS
            first = jnp.concatenate([first, first], axis=1)
            key_rows = kvbuf[k, c0:c0 + count, 0:ROWS, :].reshape(count * ROWS, HD)
            value_rows = kvbuf[k, c0:c0 + count, ROWS:2 * ROWS, :].reshape(count * ROWS, HD)
            vt[:, :count * ROWS] = dot_nt(eye, value_rows).astype(BF16)
            last = (q - c0) * ROWS + lax.broadcasted_iota(jnp.int32, (1, ROWS), 1)
            last = jnp.concatenate([last, last], axis=1)
            opening = k == 0 and c0 == 0
            tiles = count * ROWS // TILE

            def scores(hp, j, top):
                part = dot_nt(key_rows[j * TILE:(j + 1) * TILE], qrows[hp * WIDE:(hp + 1) * WIDE, :])
                pos = lax.broadcasted_iota(jnp.int32, part.shape, 0) + j * TILE
                allowed = pos >= first
                if k == 0:
                    allowed = allowed & (pos <= last)
                part = jnp.where(allowed, part, MASKED)
                s_ref[hp % 2, j * TILE:(j + 1) * TILE, :] = part
                part = jnp.max(part.reshape(TILE // 8, 8, WIDE), axis=0)
                return part if top is None else jnp.maximum(top, part)

            top = None
            for j in range(tiles):
                top = scores(0, j, top)
            for hp in range(PAIRS):
                top = jnp.max(top, axis=0, keepdims=True)
                if not opening:
                    old = m_ref[hp]
                    top = jnp.maximum(top, old)
                    factor = jnp.exp2((old - top) * EXP2_SCALE)
                total, mixed, ahead = None, None, None
                for j in range(tiles):
                    rows = slice(j * TILE, (j + 1) * TILE)
                    weights = jnp.exp2((s_ref[hp % 2, rows, :] - top) * EXP2_SCALE)
                    if hp + 1 < PAIRS:
                        ahead = scores(hp + 1, j, ahead)
                    part = jnp.sum(weights.reshape(TILE // 8, 8, WIDE), axis=0)
                    total = part if total is None else total + part
                    part = dot_nn(vt[:, rows], weights.astype(BF16))
                    mixed = part if mixed is None else mixed + part
                total = jnp.sum(total, axis=0, keepdims=True)
                if not opening:
                    total = total + l_ref[hp] * factor
                    mixed = mixed + acc[hp] * factor
                m_ref[hp] = top
                l_ref[hp] = total
                acc[hp] = mixed
                top = ahead

        guarded(cond, body)

    def teach(k):
        seg_wait(k)
        if k == 0:
            teacher(0, 0, 4)
            teacher(0, 4, 4, lambda: q >= 4)
        elif k == 4:
            teacher(4, 4, 4, lambda: z >= 4)
            teacher(4, 0, 4, lambda: (z >= 4) & (q < 4))
        else:
            teacher(k, 0, NQ, lambda: z >= k)

    def student():
        ck[...] = cartbuf[:, :, 0].reshape(SL, HD)
        cv[...] = cartbuf[:, :, 1].reshape(SL, HD)
        cvt[...] = dot_nt(eye, cv[...]).astype(BF16)
        swap = swap_matrix()
        tiles = SL // TILE

        def logits(hp, j, top):
            part = dot_nt(ck[j * TILE:(j + 1) * TILE, :], qrows[hp * WIDE:(hp + 1) * WIDE, :])
            s_ref[hp % 2, j * TILE:(j + 1) * TILE, :] = part
            part = jnp.max(part.reshape(TILE // 8, 8, WIDE), axis=0)
            return part if top is None else jnp.maximum(top, part)

        def probabilities(hp, j, inverse, out):
            rows, cols = slice(j * TILE, (j + 1) * TILE), slice(hp * WIDE, (hp + 1) * WIDE)
            probs = p_ref[rows, cols] * inverse
            p_ref[rows, cols] = probs
            low = probs.astype(BF16)
            plow[rows, cols] = low
            part = dot_nn(cvt[:, rows], low)
            return part if out is None else out + part

        top, inverse = None, None
        for j in range(tiles):
            top = logits(0, j, top)
        for hp in range(PAIRS + 1):
            if hp < PAIRS:
                top = jnp.max(top, axis=0, keepdims=True)
            total, ahead, out = None, None, None
            for j in range(tiles):
                rows, cols = slice(j * TILE, (j + 1) * TILE), slice(hp * WIDE, (hp + 1) * WIDE)
                if hp < PAIRS:
                    expo = jnp.exp2((s_ref[hp % 2, rows, :] - top) * EXP2_SCALE)
                    p_ref[rows, cols] = expo
                    part = jnp.sum(expo.reshape(TILE // 8, 8, WIDE), axis=0)
                    total = part if total is None else total + part
                if hp + 1 < PAIRS:
                    ahead = logits(hp + 1, j, ahead)
                if hp > 0:
                    out = probabilities(hp - 1, j, inverse, out)
            if hp > 0:
                ot_ref[:, (hp - 1) * WIDE:hp * WIDE] = out
                out_low = out.astype(BF16)
                for g in range(2):
                    h = (hp - 1) * 2 + g
                    rows = dot_nt(swap, out_low[:, g * ROWS:(g + 1) * ROWS])
                    sbuf[:, :, h * HD:(h + 1) * HD] = rows.astype(BF16).reshape(NQ, 16, HD)
            if hp < PAIRS:
                inverse = 1.0 / jnp.sum(total, axis=0, keepdims=True)
            top = ahead

    def exchange1():
        for r in range(1, NQ):
            send(lambda r=r: (sbuf.at[rem(q + r, NQ)], rbuf1.at[q], a1_sem.at[q]),
                 lambda r=r: (ctx(z, rem(q + r, NQ)), d))

    def exchange2():
        for r in range(1, NQ):
            recv(lambda r=r: (rbuf1.at[rem(q + r, NQ)], a1_sem.at[rem(q + r, NQ)]))
        rbuf1[q] = sbuf[q]
        swap = swap_matrix()
        s2buf[...] = dot_nn(swap, rbuf1[...].reshape(ROWS, 1024)).astype(BF16).reshape(NQ, 16, 1024)
        for r in range(1, NZ):
            send(lambda r=r: (s2buf.at[plane(r)], rbuf2.at[z], a2_sem.at[z]),
                 lambda r=r: (ctx(z + r, q), d))

    def exchange3():
        for r in range(1, NZ):
            recv(lambda r=r: (rbuf2.at[plane(r)], a2_sem.at[plane(r)]))
        rbuf2[z] = s2buf[z]
        s_out[...] = rbuf2[...].reshape(NZ * 16, 1024)

    def difference():
        for hp in range(PAIRS):
            cols = slice(hp * WIDE, (hp + 1) * WIDE)
            low_t = (acc[hp] / l_ref[hp]).astype(BF16)
            out = ot_ref[:, cols]
            delta = (WEIGHT * (out - low_t.astype(F32))).astype(BF16)
            delta_ref[:, cols] = delta
            row_ref[:, cols] = jnp.sum(delta.astype(F32) * out, axis=0, keepdims=True)
            low_ref[:, cols] = low_t

    def teacher_rows():
        for h in range(8):
            t_out[:, h * HD:(h + 1) * HD] = dot_nt(eye, low_ref[:, h * ROWS:(h + 1) * ROWS]).astype(BF16)

    NH = 2
    HZ = NZ // NH

    def gradients(half):
        n = SL // NH
        rows = slice(half * n, (half + 1) * n)
        for hp in range(PAIRS):
            cols = slice(hp * WIDE, (hp + 1) * WIDE)
            back = dot_nn(cv[rows, :], delta_ref[:, cols])
            ds_ref[:, cols] = (p_ref[rows, cols] * (back - row_ref[:, cols])).astype(BF16)
        gv = dot_nt(plow[rows, :], delta_ref[...])
        gk = dot_nn(ds_ref[...], qrows[...])
        planes = slice(half * HZ, (half + 1) * HZ)
        gbuf[planes, :, 0] = (gk * SCALE).astype(BF16).reshape(HZ, NQ, 16, HD)
        gbuf[planes, :, 1] = gv.astype(BF16).reshape(HZ, NQ, 16, HD)

    def reduce1(half):
        planes = pl.ds(half * HZ, HZ)
        for r in range(1, NQ):
            send(lambda r=r: (gbuf.at[planes, rem(q + r, NQ)], rs1.at[q, planes], r1_sem.at[q, half]),
                 lambda r=r: (ctx(z, rem(q + r, NQ)), d))

    def reduce2(half):
        planes = pl.ds(half * HZ, HZ)
        total = gbuf[planes, q].astype(F32)
        for r in range(1, NQ):
            recv(lambda r=r: (rs1.at[rem(q + r, NQ), planes], r1_sem.at[rem(q + r, NQ), half]))
        for r in range(1, NQ):
            total = total + rs1[rem(q + r, NQ), planes].astype(F32)
        zbuf[planes] = total.astype(BF16)
        for t in range(half * HZ, (half + 1) * HZ):
            send(lambda t=t: (zbuf.at[t], rs2.at[z], r2_sem.at[z]),
                 lambda t=t: (ctx(t, q), d), lambda t=t: z != t)

    def reduce3():
        total = zbuf[z].astype(F32)
        for r in range(1, NZ):
            recv(lambda r=r: (rs2.at[plane(r)], r2_sem.at[plane(r)]))
        for r in range(1, NZ):
            total = total + rs2[plane(r)].astype(F32)
        fbuf[...] = total
        for r in range(1, NDP):
            send(lambda: (fbuf, dbuf.at[d], dp_sem.at[d]), lambda r=r: (me, rem(d + r, NDP)))
        dbuf[d] = total

    def reduce4():
        for r in range(1, NDP):
            recv(lambda r=r: (dbuf.at[rem(d + r, NDP)], dp_sem.at[rem(d + r, NDP)]))
        for s in range(NDP):
            gk_out[:, s * HD:(s + 1) * HD] = dbuf[s, 0]
            gv_out[:, s * HD:(s + 1) * HD] = dbuf[s, 1]

    def finish(upto=None):
        upto = len(sent) if upto is None else upto
        for cond, make in sent[done[0]:upto]:
            guarded(cond, lambda: make().wait_send())
        done[0] = upto

    have = lambda k, part: part(k) if k < NP else None
    greet()
    own = own_copies()
    for c in own:
        c.start()
    asked = query_copies()
    for c in asked:
        c.start()
    prepare()
    for c in own:
        c.wait()
    pl.semaphore_wait(barrier, NQ - 1 + len(near) + NDP - 1)
    for steps in (1, 2):
        if steps < NP:
            z_send(0, steps)
    seg_start()
    cart_start()
    round0(0)
    for c in asked:
        c.wait()
    seg_spread()
    have(1, z_recv)
    have(1, round0)
    have(2, z_recv)
    have(2, round0)
    cart_spread()
    round1(0)
    if NP > 2:
        seg_relay()
    have(1, round1)
    have(3, z_recv)
    have(3, round0)
    have(4, z_recv)
    have(4, round0)
    round2(0)
    teach(0)
    have(2, round1)
    cart_relay()
    have(1, round2)
    have(1, teach)
    have(3, round1)
    cart_wait()
    student()
    exchange1()
    for k in (2, 3, 4):
        have(k, round2)
        have(k, teach)
    early = len(sent)
    difference()
    gradients(0)
    reduce1(0)
    gradients(1)
    reduce1(1)
    exchange2()
    teacher_rows()
    finish(early)
    reduce2(0)
    reduce2(1)
    reduce3()
    exchange3()
    reduce4()
    finish()


def write_out(t_ref, s_ref, gk_ref, gv_ref, t_hbm, s_hbm, gk_hbm, gv_hbm, sem):
    pairs = ((t_ref, t_hbm), (s_ref, s_hbm), (gk_ref, gk_hbm), (gv_ref, gv_hbm))
    copies = [pltpu.make_async_copy(a, b, sem.at[i]) for i, (a, b) in enumerate(pairs)]
    for c in copies:
        c.start()
    for c in copies:
        c.wait()


def per_device(NZ, NDP, queries, keys, values, segment_ids, cart_keys, cart_values):
    NP = min(5, NZ)
    SL = NZ * NQ * 16
    V = pltpu.VMEM
    D = pltpu.SemaphoreType.DMA
    vmem = pl.BlockSpec(memory_space=pltpu.VMEM)
    hbm = pl.BlockSpec(memory_space=pl.ANY)
    shapes = [
        jax.ShapeDtypeStruct((ROWS, 1024), BF16),
        jax.ShapeDtypeStruct((NZ * 16, 1024), BF16),
        jax.ShapeDtypeStruct((16, NDP * HD), F32),
        jax.ShapeDtypeStruct((16, NDP * HD), F32),
    ]
    results = pl.pallas_call(
        functools.partial(kernel, NZ, NDP),
        out_shape=[pltpu.VMEM(a.shape, a.dtype) for a in shapes],
        in_specs=[hbm] * 6,
        out_specs=[vmem] * 4,
        scratch_shapes=[
            V((NP, NQ, 2 * ROWS, HD), BF16),
            V((NP, NQ, 1, ROWS), jnp.int32),
            V((NZ, NQ, 2, 16, HD), BF16),
            V((1024, HD), BF16),
            V((HD, NQ * ROWS), BF16),
            V((SL, HD), BF16),
            V((SL, HD), BF16),
            V((HD, SL), BF16),
            V((PAIRS, 1, WIDE), F32),
            V((PAIRS, 1, WIDE), F32),
            V((PAIRS, HD, WIDE), F32),
            V((SL, 1024), F32),
            V((SL, 1024), BF16),
            V((HD, 1024), F32),
            V((HD, 1024), BF16),
            V((1, 1024), F32),
            V((SL // 2, 1024), BF16),
            V((2, NQ * ROWS, WIDE), F32),
            V((HD, 1024), BF16),
            V((NQ, 16, 1024), BF16),
            V((NQ, 16, 1024), BF16),
            V((NQ, 16, 1024), BF16),
            V((NZ, 16, 1024), BF16),
            V((NZ, NQ, 2, 16, HD), BF16),
            V((NQ, NZ, 2, 16, HD), BF16),
            V((NZ, 2, 16, HD), BF16),
            V((NZ, 2, 16, HD), BF16),
            V((2, 16, HD), F32),
            V((NDP, 2, 16, HD), F32),
            D((13,)), D((160,)), D((NP,)), D((NP, NQ, 2)), D((NQ,)), D((NP,)), D((NQ,)), D((NZ, 2)),
            D((NQ,)), D((NZ,)), D((NQ, 2)), D((NZ,)), D((NDP,)),
        ],
        compiler_params=pltpu.CompilerParams(
            collective_id=0, has_side_effects=True, vmem_limit_bytes=60 * 1024 * 1024
        ),
        name="distill",
    )(queries, keys, values, segment_ids.reshape(1, ROWS), cart_keys, cart_values)
    results = [pltpu.with_memory_space_constraint(a, pltpu.VMEM) for a in results]
    return pl.pallas_call(
        write_out, out_shape=shapes, in_specs=[vmem] * 4, out_specs=[hbm] * 4,
        scratch_shapes=[D((4,))], name="write_out",
    )(*results)


def solution(mesh):
    nz, ndp = mesh.shape["ctx"] // NQ, mesh.shape["dp"]
    specs = (
        P("ctx", "dp"), P("ctx", "dp"), P("ctx", "dp"), P("ctx"), P("ctx", "dp"), P("ctx", "dp"),
    )
    return jax.shard_map(
        functools.partial(per_device, nz, ndp), mesh=mesh, in_specs=specs,
        out_specs=(P("ctx", "dp"), P("ctx", "dp"), P("ctx", None), P("ctx", None)),
        check_vma=False,
    )
```
